32 devices in a mesh: ta: 8 (over y, x, core), ba: 4 (over z).
Axes of the slice: x: 2, y: 2, z: 4, core: 2. Of those that a mesh axis runs over, the one named last changes fastest.
Arguments:
- search_block: float32 [16, 2, 4, 3, 16, 512], P(None, None, None, None, 'ta'), may hold values from -140 to 140
- kept_basis: float32 [128, 2, 4, 3, 16, 512], P('ba', None, None, None, 'ta'), may hold values from -4 to 4
- gauge_links: float32 [4, 2, 3, 3, 16, 512], P(None, None, None, None, 'ta'), may hold values from -1 to 1, as said below
- clover_term: float32 [2, 2, 6, 6, 16, 512], P(None, None, None, None, 'ta'), may hold values from -0.5 to 1.3, as said below
Outputs:
- ortho_block: float32 [16, 2, 4, 3, 16, 512], P('ba', None, None, None, 'ta')
- correlations: float32 [2, 128, 16], P(None, 'ba')
The draws below stay inside these ranges and needn't reach their ends.
Inputs may be any that keep to these rules, and one draw needn't show every extreme that they name: `gauge_links`: every link matrix is special unitary. `clover_term`: each 6x6 block of the clover term is Hermitian.
All inputs are finite; a program needn't handle non-finite values.
Results may differ from the reference program's by a relative error of at most 0.0002.
Values sent between devices are 32-bit elements; how exact they have to be, the bound alone decides.
No kernel may reach another device: no remote copies, remote signals or barrier semaphores. Data moves between devices by JAX's collectives and lax.ppermute only.
A program may use at most 128 MiB of HBM per device.

```python
import math
import jax
import jax.numpy as jnp
import numpy as np
from jax import lax

BLOCK = 16
KEPT = 128
LS = 8
NT = 16


def basis_values(key):
    base_key = jax.random.fold_in(key, 101)
    draw_shape = (KEPT, 2, 4, 3, NT, LS ** 3)
    return jax.random.truncated_normal(base_key, -4.0, 4.0, draw_shape, jnp.float32)


def draw_kept_basis(key, part):
    return basis_values(key)


def draw_search_block(key, part):
    kept_values = basis_values(key)
    chosen = jax.random.permutation(jax.random.fold_in(key, 202), KEPT)[:BLOCK]
    site_count = LS ** 3
    noise = jax.random.truncated_normal(jax.random.fold_in(key, 203), -4.0, 4.0, (BLOCK, 2, 4, 3, NT, site_count), jnp.float32)
    time_index = jnp.arange(NT, dtype=jnp.float32)
    ramp = jnp.exp(math.log(3.0) * time_index / max(NT - 1, 1)) / math.sqrt(3.0)
    spread = math.log(4.0)
    mixed = 0.8 * kept_values[chosen] + 0.6 * noise
    row_scale = jnp.exp(spread * (jax.random.uniform(jax.random.fold_in(key, 205), (1, 1, 1, 1, NT, site_count), jnp.float32) - 0.5))
    column_scale = jnp.exp(spread * (jax.random.uniform(jax.random.fold_in(key, 206), (BLOCK, 1, 1, 1, 1, 1), jnp.float32) - 0.5))
    return mixed * row_scale * column_scale * ramp[:, None]


def embedded(key, first, second):
    draw_shape = (4, NT, LS ** 3)
    angle_theta = jax.random.uniform(jax.random.fold_in(key, 1), draw_shape, jnp.float32, 0.0, 2.0 * math.pi)
    angle_alpha = jax.random.uniform(jax.random.fold_in(key, 2), draw_shape, jnp.float32, 0.0, 2.0 * math.pi)
    angle_beta = jax.random.uniform(jax.random.fold_in(key, 3), draw_shape, jnp.float32, 0.0, 2.0 * math.pi)
    diag_re = jnp.cos(angle_theta) * jnp.cos(angle_alpha)
    diag_im = jnp.cos(angle_theta) * jnp.sin(angle_alpha)
    off_re = jnp.sin(angle_theta) * jnp.cos(angle_beta)
    off_im = jnp.sin(angle_theta) * jnp.sin(angle_beta)
    identity = jnp.broadcast_to(jnp.eye(3, dtype=jnp.float32)[:, :, None, None, None], (3, 3) + draw_shape)
    mat_re = identity.at[first, first].set(diag_re).at[first, second].set(off_re).at[second, first].set(-off_re).at[second, second].set(diag_re)
    mat_im = jnp.zeros_like(identity).at[first, first].set(diag_im).at[first, second].set(off_im).at[second, first].set(off_im).at[second, second].set(-diag_im)
    return (mat_re, mat_im)


def matrix_product(left_re, left_im, right_re, right_im):
    out_re = jnp.sum(left_re[:, :, None] * right_re[None] - left_im[:, :, None] * right_im[None], axis=1)
    out_im = jnp.sum(left_re[:, :, None] * right_im[None] + left_im[:, :, None] * right_re[None], axis=1)
    return (out_re, out_im)


def draw_gauge_links(key, part):
    first_re, first_im = embedded(jax.random.fold_in(key, 11), 0, 1)
    second_re, second_im = embedded(jax.random.fold_in(key, 12), 1, 2)
    third_re, third_im = embedded(jax.random.fold_in(key, 13), 0, 2)
    step_re, step_im = matrix_product(first_re, first_im, second_re, second_im)
    final_re, final_im = matrix_product(step_re, step_im, third_re, third_im)
    stacked = jnp.stack([final_re, final_im], 0)
    return jnp.transpose(stacked, (3, 0, 1, 2, 4, 5))


def draw_clover_term(key, part):
    site_count = LS ** 3
    draw_shape = (2, 6, 6, NT, site_count)
    raw_re = 0.15 * jax.random.truncated_normal(jax.random.fold_in(key, 31), -2.0, 2.0, draw_shape, jnp.float32)
    raw_im = 0.15 * jax.random.truncated_normal(jax.random.fold_in(key, 32), -2.0, 2.0, draw_shape, jnp.float32)
    symmetric_re = 0.5 * (raw_re + raw_re.swapaxes(1, 2))
    antisym_im = 0.5 * (raw_im - raw_im.swapaxes(1, 2))
    diagonal = jax.random.uniform(jax.random.fold_in(key, 33), (2, 6, NT, site_count), jnp.float32, 0.7, 1.3)
    eye_six = jnp.eye(6, dtype=jnp.float32)[None, :, :, None, None]
    hermit_re = symmetric_re * (1.0 - eye_six) + eye_six * diagonal[:, :, None]
    return jnp.stack([hermit_re, antisym_im], 1)


def setup_inputs(seed: int = 0) -> dict:
    arg_keys = jax.random.split(jax.random.key(seed), 5)
    search_block = draw_search_block(jax.random.fold_in(arg_keys[4], 71), 0)
    kept_basis = draw_kept_basis(jax.random.fold_in(arg_keys[4], 71), 0)
    gauge_links = draw_gauge_links(jax.random.fold_in(arg_keys[4], 71), 0)
    clover_term = draw_clover_term(jax.random.fold_in(arg_keys[4], 71), 0)
    return dict(search_block=search_block, kept_basis=kept_basis, gauge_links=gauge_links, clover_term=clover_term)


HOPPING = 0.13
HIGHEST = lax.Precision.HIGHEST

def gamma_tables():
    gamma_re = np.zeros((4, 4, 4), np.float32)
    gamma_im = np.zeros((4, 4, 4), np.float32)
    gamma_im[0, 0:2, 2:4] = [[0, -1], [-1, 0]]
    gamma_im[0, 2:4, 0:2] = [[0, 1], [1, 0]]
    gamma_re[1, 0:2, 2:4] = [[0, -1], [1, 0]]
    gamma_re[1, 2:4, 0:2] = [[0, 1], [-1, 0]]
    gamma_im[2, 0:2, 2:4] = [[-1, 0], [0, 1]]
    gamma_im[2, 2:4, 0:2] = [[1, 0], [0, -1]]
    gamma_re[3, 0:2, 2:4] = np.eye(2)
    gamma_re[3, 2:4, 0:2] = np.eye(2)
    return (gamma_re, gamma_im)

def gamma_apply(direction, spinor):
    tables_re, tables_im = gamma_tables()
    field_re = spinor[:, 0]
    field_im = spinor[:, 1]
    out_re = jnp.zeros_like(field_re)
    out_im = jnp.zeros_like(field_im)
    if np.any(tables_re[direction]):
        matrix = jnp.asarray(tables_re[direction])
        out_re = out_re + jnp.einsum('as,vsctx->vactx', matrix, field_re, precision=HIGHEST)
        out_im = out_im + jnp.einsum('as,vsctx->vactx', matrix, field_im, precision=HIGHEST)
    if np.any(tables_im[direction]):
        matrix = jnp.asarray(tables_im[direction])
        out_re = out_re - jnp.einsum('as,vsctx->vactx', matrix, field_im, precision=HIGHEST)
        out_im = out_im + jnp.einsum('as,vsctx->vactx', matrix, field_re, precision=HIGHEST)
    return jnp.stack([out_re, out_im], 1)

def gamma_five(spinor):
    return jnp.concatenate([spinor[:, :, :2], -spinor[:, :, 2:]], axis=2)

def colour(link_dir, spinor):
    link_re = link_dir[0][None, None]
    link_im = link_dir[1][None, None]
    field_re = spinor[:, 0][:, :, None]
    field_im = spinor[:, 1][:, :, None]
    out_re = lax.optimization_barrier(jnp.sum(link_re * field_re - link_im * field_im, axis=3))
    out_im = lax.optimization_barrier(jnp.sum(link_re * field_im + link_im * field_re, axis=3))
    return jnp.stack([out_re, out_im], 1)

def dagger(link_dir):
    return jnp.stack([link_dir[0].swapaxes(0, 1), -link_dir[1].swapaxes(0, 1)], 0)

def shift_space(values, stride, forward):
    coordinate = jnp.arange(values.shape[-1]) // stride % LS
    if forward:
        return jnp.where(coordinate == LS - 1, jnp.roll(values, (LS - 1) * stride, axis=-1), jnp.roll(values, -stride, axis=-1))
    return jnp.where(coordinate == 0, jnp.roll(values, -(LS - 1) * stride, axis=-1), jnp.roll(values, stride, axis=-1))

def space_hops(spinor, link_field):
    hop_total = jnp.zeros_like(spinor)
    strides = (LS * LS, LS, 1)
    for direction in range(3):
        stride = strides[direction]
        link_dir = link_field[direction]
        ahead_term = colour(link_dir, shift_space(spinor, stride, True))
        behind = colour(dagger(shift_space(link_dir, stride, False)), shift_space(spinor, stride, False))
        hop_total = hop_total + (ahead_term + behind) - gamma_apply(direction, ahead_term - behind)
    return hop_total

def clover_apply(clover, spinor):
    vectors = spinor.shape[0]
    pieces = []
    for chiral in range(2):
        chiral_part = spinor[:, :, 2 * chiral:2 * chiral + 2]
        flat_part = chiral_part.reshape(vectors, 2, 6, chiral_part.shape[-2], chiral_part.shape[-1])
        mat_re = clover[chiral, 0][None]
        mat_im = clover[chiral, 1][None]
        vec_re = flat_part[:, 0][:, None]
        vec_im = flat_part[:, 1][:, None]
        out_re = lax.optimization_barrier(jnp.sum(mat_re * vec_re - mat_im * vec_im, axis=2))
        out_im = lax.optimization_barrier(jnp.sum(mat_re * vec_im + mat_im * vec_re, axis=2))
        pieces.append(jnp.stack([out_re, out_im], 1).reshape(chiral_part.shape))
    return jnp.concatenate(pieces, axis=2)

def dirac_apply(spinor, link_field, clover):
    slices = spinor.shape[4]
    time_index = jnp.arange(slices)
    sign_ahead = jnp.where(time_index == slices - 1, -1.0, 1.0).astype(spinor.dtype)
    sign_behind = jnp.where(time_index == 0, -1.0, 1.0).astype(spinor.dtype)
    ahead_field = jnp.roll(spinor, -1, axis=4) * sign_ahead[:, None]
    behind_field = jnp.roll(spinor, 1, axis=4) * sign_behind[:, None]
    link_time = link_field[3]
    ahead_term = colour(link_time, ahead_field)
    behind = colour(dagger(jnp.roll(link_time, 1, axis=3)), behind_field)
    hops = space_hops(spinor, link_field) + (ahead_term + behind) - gamma_apply(3, ahead_term - behind)
    return clover_apply(clover, spinor) - HOPPING * hops

def inner_product(left_re, left_im, right_re, right_im, norm_scale):
    real_part = jnp.einsum('kcn,jcn->kj', left_re, right_re, precision=HIGHEST) + jnp.einsum('kcn,jcn->kj', left_im, right_im, precision=HIGHEST)
    imag_part = jnp.einsum('kcn,jcn->kj', left_re, right_im, precision=HIGHEST) - jnp.einsum('kcn,jcn->kj', left_im, right_re, precision=HIGHEST)
    return (real_part * norm_scale, imag_part * norm_scale)

def combine_basis(coef_re, coef_im, vec_re, vec_im):
    out_re = jnp.einsum('kj,kcn->jcn', coef_re, vec_re, precision=HIGHEST) - jnp.einsum('kj,kcn->jcn', coef_im, vec_im, precision=HIGHEST)
    out_im = jnp.einsum('kj,kcn->jcn', coef_im, vec_re, precision=HIGHEST) + jnp.einsum('kj,kcn->jcn', coef_re, vec_im, precision=HIGHEST)
    return (out_re, out_im)

def cholesky_complex(gram_re, gram_im):
    matrix_order = gram_re.shape[0]
    lower_re = jnp.zeros_like(gram_re)
    lower_im = jnp.zeros_like(gram_im)
    index_row = jnp.arange(matrix_order)
    for column in range(matrix_order):
        row_re = lower_re[column]
        row_im = lower_im[column]
        acc_re = gram_re[:, column] - lax.optimization_barrier(jnp.sum(lower_re * row_re[None, :] + lower_im * row_im[None, :], axis=1))
        acc_im = gram_im[:, column] - lax.optimization_barrier(jnp.sum(lower_im * row_re[None, :] - lower_re * row_im[None, :], axis=1))
        pivot_value = jnp.sqrt(acc_re[column])
        below_mask = index_row > column
        new_re = jnp.where(index_row == column, pivot_value, jnp.where(below_mask, acc_re / pivot_value, 0.0))
        new_im = jnp.where(below_mask, acc_im / pivot_value, 0.0)
        lower_re = lower_re.at[:, column].set(new_re)
        lower_im = lower_im.at[:, column].set(new_im)
    return (lower_re, lower_im)

def invert_lower(lower_re, lower_im):
    matrix_order = lower_re.shape[0]
    inverse_re = jnp.zeros_like(lower_re)
    inverse_im = jnp.zeros_like(lower_im)
    index_row = jnp.arange(matrix_order)
    for row_index in range(matrix_order):
        row_re = lower_re[row_index]
        row_im = lower_im[row_index]
        sum_re = lax.optimization_barrier(jnp.sum(row_re[:, None] * inverse_re - row_im[:, None] * inverse_im, axis=0))
        sum_im = lax.optimization_barrier(jnp.sum(row_re[:, None] * inverse_im + row_im[:, None] * inverse_re, axis=0))
        unit_row = jnp.where(index_row == row_index, 1.0, 0.0).astype(lower_re.dtype)
        pivot_value = lower_re[row_index, row_index]
        inverse_re = inverse_re.at[row_index].set((unit_row - sum_re) / pivot_value)
        inverse_im = inverse_im.at[row_index].set(-sum_im / pivot_value)
    return (inverse_re, inverse_im)

def reference(search_block, kept_basis, gauge_links, clover_term):
    first_apply = dirac_apply(search_block, gauge_links, clover_term)
    applied = gamma_five(dirac_apply(gamma_five(first_apply), gauge_links, clover_term))
    block_size = search_block.shape[0]
    kept_size = kept_basis.shape[0]
    site_count = search_block.shape[4] * search_block.shape[5]
    norm_scale = 1.0 / (24.0 * site_count)
    applied_re = applied[:, 0].reshape(block_size, 12, site_count)
    applied_im = applied[:, 1].reshape(block_size, 12, site_count)
    basis_re = kept_basis[:, 0].reshape(kept_size, 12, site_count)
    basis_im = kept_basis[:, 1].reshape(kept_size, 12, site_count)
    over_re, over_im = inner_product(basis_re, basis_im, applied_re, applied_im, norm_scale)
    proj_re, proj_im = combine_basis(over_re, over_im, basis_re, basis_im)
    rest_re = applied_re - proj_re
    rest_im = applied_im - proj_im
    gram_re, gram_im = inner_product(rest_re, rest_im, rest_re, rest_im, norm_scale)
    lower_re, lower_im = cholesky_complex(gram_re, gram_im)
    inverse_re, inverse_im = invert_lower(lower_re, lower_im)
    ortho_re, ortho_im = combine_basis(inverse_re.T, -inverse_im.T, rest_re, rest_im)
    ortho_out = jnp.stack([ortho_re, ortho_im], 1).reshape(search_block.shape)
    return (ortho_out, jnp.stack([over_re, over_im], 0))
```

```python
import functools
import math

import jax
import jax.numpy as jnp
from jax import lax
from jax.experimental import pallas as pl
from jax.experimental.pallas import tpu as pltpu
from jax.sharding import PartitionSpec as P

HOPPING = 0.13
LANES = 128
COMPS = 12
PROJECT = (
    ((1, 1), (0, 1)),
    ((1, 0), (0, 2)),
    ((0, 1), (1, 3)),
    ((0, 2), (1, 2)),
)
REBUILD = (
    ((1, 3), (0, 3)),
    ((1, 0), (0, 2)),
    ((0, 3), (1, 1)),
    ((0, 2), (1, 2)),
)


def add_phase(left, right, phase):
    a, b = left
    c, d = right
    phase %= 4
    if phase == 0:
        return a + c, b + d
    if phase == 1:
        return a - d, b + c
    if phase == 2:
        return a - c, b - d
    return a + d, b - c


def plus(left, right):
    return left[0] + right[0], left[1] + right[1]


def minus(left, right):
    return left[0] - right[0], left[1] - right[1]


def rolled(value, shift, axis):
    shift %= value.shape[axis]
    return pltpu.roll(value, shift, axis) if shift else value


class Lattice:
    def __init__(self, slices, sites):
        self.slices = slices
        self.side = round(sites ** (1 / 3))
        self.rows = slices * sites // LANES
        self.shape = (self.rows, LANES)
        if self.side**3 != sites or LANES % (self.side * self.side) or COMPS % slices:
            raise ValueError("lattice shape")

    def masks(self):
        lane = lax.broadcasted_iota(jnp.int32, self.shape, 1)
        row = lax.broadcasted_iota(jnp.int32, self.shape, 0)
        side = self.side
        self.time = row % self.slices
        self.x_low = lane // (side * side)
        self.y = lane // side % side
        self.z = lane % side

    def shift(self, value, direction, ahead):
        side, area = self.side, self.side * self.side
        if direction == 0:
            step = 1 if ahead else -1
            edge = self.x_low == (0 if ahead else LANES // area - 1)
            mixed = jnp.where(edge, rolled(value, -step * self.slices, 0), value)
            return rolled(mixed, -step * area, 1)
        if direction < 3:
            place, unit = (self.y, side) if direction == 1 else (self.z, 1)
            edge = place == (side - 1 if ahead else 0)
            step = unit if ahead else -unit
            return jnp.where(
                edge, rolled(value, (side - 1) * step, 1), rolled(value, -step, 1)
            )
        if ahead:
            return jnp.where(self.time == self.slices - 1, 0.0, rolled(value, -1, 0))
        return jnp.where(self.time == 0, 0.0, rolled(value, 1, 0))


def load_spinor(ref, vector):
    def at(spin, colour):
        place = vector * (2 * COMPS) + spin * 3 + colour
        return ref[place], ref[place + COMPS]

    return at


def link_at(links, direction):
    def at(row, column):
        place = direction * 18 + row * 3 + column
        return links[place], links[place + 9]

    return at


def times_link(link, half):
    out = []
    for row in range(3):
        re = im = None
        for column in range(3):
            u, v = link(row, column)
            a, b = half[column]
            re = u * a - v * b if re is None else re + u * a - v * b
            im = u * b + v * a if im is None else im + u * b + v * a
        out.append((re, im))
    return out


def times_dagger(link, half):
    out = []
    for row in range(3):
        re = im = None
        for column in range(3):
            u, v = link(column, row)
            a, b = half[column]
            re = u * a + v * b if re is None else re + u * a + v * b
            im = u * b - v * a if im is None else im + u * b - v * a
        out.append((re, im))
    return out


def half_spinor(spinor, direction, spin, ahead):
    other, phase = PROJECT[direction][spin]
    phase = phase if ahead else phase + 2
    return [add_phase(spinor(spin, c), spinor(2 + other, c), phase) for c in range(3)]


def pack_rim(lattice, spinor, links, ahead_ref, behind_ref, vector):
    slices = lattice.slices
    ahead, behind = [], []
    for spin in range(2):
        ahead += half_spinor(spinor, 3, spin, True)
        behind += times_dagger(link_at(links, 3), half_spinor(spinor, 3, spin, False))
    for values, origin, ref in ((ahead, 0, ahead_ref), (behind, slices - 1, behind_ref)):
        flat = [part for pair in values for part in pair]
        for group in range(COMPS // slices):
            tile = None
            for place in range(slices):
                moved = rolled(flat[group * slices + place], place - origin, 0)
                tile = moved if tile is None else jnp.where(lattice.time == place, moved, tile)
            ref[vector * (COMPS // slices) + group] = tile


def unpack_rim(lattice, ref, vector, ahead, sign):
    slices = lattice.slices
    target = slices - 1 if ahead else 0
    flat = []
    for comp in range(COMPS):
        tile = ref[vector * (COMPS // slices) + comp // slices]
        moved = rolled(tile, target - comp % slices, 0)
        flat.append(jnp.where(lattice.time == target, moved * sign, 0.0))
    return [(flat[2 * i], flat[2 * i + 1]) for i in range(COMPS // 2)]


def pack_kernel(lattice, vectors, psi, links, ahead_ref, behind_ref):
    lattice.masks()

    def body(vector, carry):
        pack_rim(lattice, load_spinor(psi, vector), links, ahead_ref, behind_ref, vector)
        return carry

    lax.fori_loop(0, vectors, body, 0)


def local_kernel(lattice, vectors, psi, links, clover, out):
    lattice.masks()

    def body(vector, carry):
        spinor = load_spinor(psi, vector)
        upper = [[None] * 3 for _ in range(2)]
        lower = [[None] * 3 for _ in range(2)]
        for direction in range(4):
            link = link_at(links, direction)
            for spin in range(2):
                half = half_spinor(spinor, direction, spin, True)
                half = [tuple(lattice.shift(p, direction, True) for p in h) for h in half]
                ahead = times_link(link, half)
                half = half_spinor(spinor, direction, spin, False)
                behind = times_dagger(link, half)
                behind = [tuple(lattice.shift(p, direction, False) for p in h) for h in behind]
                place, phase = REBUILD[direction][spin]
                for c in range(3):
                    total, diff = plus(ahead[c], behind[c]), minus(ahead[c], behind[c])
                    if upper[spin][c] is None:
                        upper[spin][c] = total
                    else:
                        upper[spin][c] = plus(upper[spin][c], total)
                    if lower[place][c] is None:
                        zero = jnp.zeros_like(diff[0])
                        lower[place][c] = add_phase((zero, zero), diff, phase)
                    else:
                        lower[place][c] = add_phase(lower[place][c], diff, phase)
        for chiral, hops in ((0, upper), (1, lower)):
            for row in range(6):
                re = im = None
                for column in range(6):
                    place = chiral * 72 + row * 6 + column
                    u, v = clover[place], clover[place + 36]
                    a, b = spinor(2 * chiral + column // 3, column % 3)
                    re = u * a - v * b if re is None else re + u * a - v * b
                    im = u * b + v * a if im is None else im + u * b + v * a
                place = vector * (2 * COMPS) + chiral * 6 + row
                out[place] = re - HOPPING * hops[row // 3][row % 3][0]
                out[place + COMPS] = im - HOPPING * hops[row // 3][row % 3][1]
        return carry

    lax.fori_loop(0, vectors, body, 0)


def rim_signs():
    count, here = lax.axis_size("ta"), lax.axis_index("ta")
    one = jnp.float32(1.0)
    return jnp.where(here == count - 1, -one, one), jnp.where(here == 0, -one, one)


def finish(lattice, links, part, rim_ahead, rim_behind, vector, signs, store):
    ahead_all = unpack_rim(lattice, rim_ahead, vector, True, signs[0])
    behind_all = unpack_rim(lattice, rim_behind, vector, False, signs[1])
    for spin in range(2):
        ahead = times_link(link_at(links, 3), ahead_all[3 * spin : 3 * spin + 3])
        behind = behind_all[3 * spin : 3 * spin + 3]
        for c in range(3):
            for ri in range(2):
                f, b = ahead[c][ri], behind[c][ri]
                place = vector * (2 * COMPS) + ri * COMPS + spin * 3 + c
                store(place, part[place] - HOPPING * (f + b))
                store(place + 6, -(part[place + 6] + HOPPING * (f - b)))


def middle_kernel(
    lattice, vectors, part, links, rim_ahead, rim_behind, out, ahead_ref, behind_ref
):
    lattice.masks()
    signs = rim_signs()

    def body(vector, carry):
        values = {}

        def store(place, value):
            out[place] = value

        finish(lattice, links, part, rim_ahead, rim_behind, vector, signs, store)
        pack_rim(lattice, load_spinor(out, vector), links, ahead_ref, behind_ref, vector)
        return carry

    lax.fori_loop(0, vectors, body, 0)


def two_halves(value):
    high = value.astype(jnp.bfloat16)
    return high, (value - high.astype(jnp.float32)).astype(jnp.bfloat16)


def basis_kernel(groups, kept, blocks, basis, out):
    per = blocks // groups

    def body(block, carry):
        rows = jnp.concatenate(
            [
                basis[pl.ds(block, kept, stride=2 * blocks), :],
                basis[pl.ds(blocks + block, kept, stride=2 * blocks), :],
            ],
            axis=0,
        )
        high, low = two_halves(rows)
        lanes = pl.ds(pl.multiple_of(block % per * LANES, LANES), LANES)
        out[block // per, : 2 * kept, lanes] = high
        out[block // per, 2 * kept :, lanes] = low
        return carry

    lax.fori_loop(0, blocks, body, 0, unroll=2)


def correlate_kernel(
    lattice, groups, vectors, kept, blocks, scale,
    part, links, rim_ahead, rim_behind, basis, applied, over, field,
):
    lattice.masks()
    signs = rim_signs()
    rows = lattice.rows

    def body(vector, carry):
        def store(place, value):
            start = place * rows
            field[pl.ds(start if isinstance(start, int) else pl.multiple_of(start, rows), rows), :] = value

        finish(lattice, links, part, rim_ahead, rim_behind, vector, signs, store)
        return carry

    lax.fori_loop(0, vectors, body, 0)
    per = blocks // groups

    def relay(block, carry):
        lanes = pl.ds(pl.multiple_of(block % per * LANES, LANES), LANES)
        for ri in range(2):
            start = ri * blocks + block
            applied[block // per, ri * vectors : (ri + 1) * vectors, lanes] = field[
                pl.ds(start, vectors, stride=2 * blocks), :
            ]
        return carry

    lax.fori_loop(0, blocks, relay, 0, unroll=2)
    total = None
    for group in range(groups):
        both = jnp.concatenate(two_halves(applied[group]), axis=0)
        term = lax.dot_general(
            both, basis[group], (((1,), (1,)), ((), ())), preferred_element_type=jnp.float32
        )
        total = term if total is None else total + term
    total = total[: 2 * vectors] + total[2 * vectors :]
    total = total[:, : 2 * kept] + total[:, 2 * kept :]
    real, imag = total[:vectors], total[vectors:]
    over[:vectors, :] = scale * (real[:, :kept] + imag[:, kept:])
    over[vectors:, :] = scale * (imag[:, :kept] - real[:, kept:])


def partner(here, step, count):
    if count & (count - 1) == 0:
        return here ^ step
    return (here + step) % count


def source(here, step, count):
    if count & (count - 1) == 0:
        return here ^ step
    return (here + count - step) % count


def exchanged(values, axis):
    count = lax.axis_size(axis)
    out = [values[0]]
    for step in range(1, count):
        pairs = [(i, partner(i, step, count)) for i in range(count)]
        out.append(lax.ppermute(values[step], axis, pairs))
    return out


def summed(value, axis):
    count = lax.axis_size(axis)
    if count & (count - 1):
        return lax.psum(value, axis)
    step = 1
    while step < count:
        value = value + lax.ppermute(value, axis, [(i, i ^ step) for i in range(count)])
        step *= 2
    return value


def project_kernel(groups, vectors, kept, over, basis, *outs):
    here = lax.axis_index("ba")
    real, imag = over[:vectors, :], over[vectors:, :]
    weight = jnp.concatenate(
        [
            jnp.concatenate([real, -imag], axis=1),
            jnp.concatenate([imag, real], axis=1),
        ],
        axis=0,
    )
    high, low = two_halves(weight)
    weight = jnp.concatenate(
        [jnp.concatenate([high, high], axis=1), jnp.concatenate([low, low], axis=1)], axis=0
    )
    for step in range(groups):
        both = jnp.dot(
            weight, basis[partner(here, step, groups)], preferred_element_type=jnp.float32
        )
        outs[step][...] = both[: 2 * vectors] + both[2 * vectors :]


def rest_kernel(groups, vectors, scale, applied, *refs):
    parts, (rest_ref, gram) = refs[:groups], refs[groups:]
    here = lax.axis_index("ba")
    rest = applied[here]
    total = parts[0][...]
    for part in parts[1:]:
        total = total + part[...]
    rest = rest - total
    rest_ref[...] = rest
    both = jnp.concatenate(two_halves(rest), axis=0)
    full = lax.dot_general(
        both, both, (((1,), (1,)), ((), ())), preferred_element_type=jnp.float32
    )
    full = full[: 2 * vectors] + full[2 * vectors :]
    full = full[:, : 2 * vectors] + full[:, 2 * vectors :]
    real, imag = full[:vectors], full[vectors:]
    gram[:, :vectors] = scale * (real[:, :vectors] + imag[:, vectors:])
    gram[:, vectors:] = scale * (real[:, vectors:] - imag[:, :vectors])


def ortho_kernel(groups, vectors, gram, rest, *outs):
    here = lax.axis_index("ba")
    work = outs[-1]
    outs = outs[:-1]
    shape = (vectors, 2 * vectors)
    row = lax.broadcasted_iota(jnp.int32, shape, 0)
    lane = lax.broadcasted_iota(jnp.int32, shape, 1)
    unit = jnp.where(lane == row + vectors, 1.0, 0.0)
    re = jnp.where(lane < vectors, gram[...], unit)
    im = jnp.where(lane < vectors, pltpu.roll(gram[...], vectors, 1), 0.0) if False else None
    im = jnp.concatenate([gram[:, vectors:], jnp.zeros((vectors, vectors), jnp.float32)], axis=1)
    for pivot in range(vectors):
        scale = 1.0 / jnp.sqrt(re[pivot : pivot + 1, pivot : pivot + 1])
        row_re, row_im = re[pivot : pivot + 1] * scale, im[pivot : pivot + 1] * scale
        col_re, col_im = re[:, pivot : pivot + 1] * scale, im[:, pivot : pivot + 1] * scale
        below = row > pivot
        new_re = re - (col_re * row_re - col_im * row_im)
        new_im = im - (col_re * row_im + col_im * row_re)
        re = jnp.where(below, new_re, jnp.where(row == pivot, row_re, re))
        im = jnp.where(below, new_im, jnp.where(row == pivot, row_im, im))
    inv_re, inv_im = re[:, vectors:], im[:, vectors:]
    weight = jnp.concatenate(
        [
            jnp.concatenate([inv_re, inv_im], axis=1),
            jnp.concatenate([-inv_im, inv_re], axis=1),
        ],
        axis=0,
    )
    high, low = two_halves(weight)
    weight = jnp.concatenate(
        [jnp.concatenate([high, high], axis=1), jnp.concatenate([low, low], axis=1)], axis=0
    )
    both = jnp.concatenate(two_halves(rest[...]), axis=0)
    full = jnp.dot(weight, both, preferred_element_type=jnp.float32)
    full = full[: 2 * vectors] + full[2 * vectors :]
    own = vectors // groups
    for group in range(groups):
        for ri in range(2):
            start = ri * vectors + group * own
            work[group, ri * own : (ri + 1) * own, :] = full[start : start + own]
    for step in range(groups):
        outs[step][...] = work[partner(here, step, groups)]


def place_kernel(groups, own, blocks, *refs):
    parts, out = refs[:groups], refs[groups]
    here = lax.axis_index("ba")
    per = blocks // groups
    for step in range(groups):
        first = source(here, step, groups) * per
        for block in range(per):
            for ri in range(2):
                value = parts[step][ri * own : (ri + 1) * own, block * LANES : (block + 1) * LANES]
                out[pl.ds(first + block + ri * blocks, own, stride=2 * blocks), :] = value


def call(kernel, outs, *args, scratch=(), flops=0):
    nbytes = sum(a.size * a.dtype.itemsize for a in (*args, *outs))
    spec = pl.BlockSpec(memory_space=pltpu.VMEM)
    return pl.pallas_call(
        kernel,
        out_shape=tuple(outs),
        in_specs=[spec] * len(args),
        out_specs=tuple([spec] * len(outs)),
        scratch_shapes=list(scratch),
        compiler_params=pltpu.CompilerParams(vmem_limit_bytes=40 * 1024 * 1024),
        cost_estimate=pl.CostEstimate(flops=flops, bytes_accessed=nbytes, transcendentals=0),
    )(*args)


def shape_of(*dims):
    return jax.ShapeDtypeStruct(dims, jnp.float32)


def tiles_of(value, leading):
    slices, sites = value.shape[-2:]
    value = value.reshape(leading, slices, sites // LANES, LANES)
    return value.swapaxes(1, 2).reshape(leading, slices * sites // LANES, LANES)


def per_device(search_block, kept_basis, gauge_links, clover_term):
    vectors, kept = search_block.shape[0], kept_basis.shape[0]
    slices, sites = search_block.shape[-2:]
    groups, places = lax.axis_size("ba"), lax.axis_size("ta")
    lattice = Lattice(slices, sites)
    rows = lattice.rows
    blocks = COMPS * rows
    per = blocks // groups
    own = vectors // groups
    scale = 1.0 / (2 * COMPS * slices * sites * places)
    psi = tiles_of(search_block, vectors * 2 * COMPS)
    basis = tiles_of(kept_basis, kept * 2 * COMPS).reshape(kept * 2 * blocks, LANES)
    links = tiles_of(gauge_links, 72)
    clover = tiles_of(clover_term, 144)
    rim = shape_of(vectors * COMPS // slices, rows, LANES)
    field = shape_of(vectors * 2 * COMPS, rows, LANES)
    work = vectors * rows * LANES

    def swap(ahead, behind):
        down = [(i, (i + places - 1) % places) for i in range(places)]
        up = [(i, (i + 1) % places) for i in range(places)]
        return lax.ppermute(ahead, "ta", down), lax.ppermute(behind, "ta", up)

    ahead, behind = call(
        functools.partial(pack_kernel, lattice, vectors), (rim, rim), psi, links, flops=200 * work
    )
    rims = swap(ahead, behind)
    local = functools.partial(local_kernel, lattice, vectors)
    (part,) = call(local, (field,), psi, links, clover, flops=2000 * work)
    (rows_of_basis,) = call(
        functools.partial(basis_kernel, groups, kept, blocks),
        (jax.ShapeDtypeStruct((groups, 4 * kept, per * LANES), jnp.bfloat16),),
        basis,
    )
    first, ahead, behind = call(
        functools.partial(middle_kernel, lattice, vectors),
        (field, rim, rim),
        part,
        links,
        *rims,
        flops=400 * work,
    )
    rims = swap(ahead, behind)
    (part,) = call(local, (field,), first, links, clover, flops=2000 * work)
    applied, over = call(
        functools.partial(correlate_kernel, lattice, groups, vectors, kept, blocks, scale),
        (shape_of(groups, 2 * vectors, per * LANES), shape_of(2 * vectors, kept)),
        part,
        links,
        *rims,
        rows_of_basis,
        scratch=[pltpu.VMEM((vectors * 2 * blocks, LANES), jnp.float32)],
        flops=400 * work,
    )
    over = summed(over, "ta")
    quarter = shape_of(2 * vectors, per * LANES)
    parts = call(
        functools.partial(project_kernel, groups, vectors, kept),
        (quarter,) * groups,
        over,
        rows_of_basis,
    )
    parts = exchanged(parts, "ba")
    rest, gram = call(
        functools.partial(rest_kernel, groups, vectors, scale),
        (quarter, shape_of(vectors, 2 * vectors)),
        applied,
        *parts,
    )
    gram = summed(summed(gram, "ta"), "ba")
    piece = shape_of(2 * own, per * LANES)
    pieces = call(
        functools.partial(ortho_kernel, groups, vectors),
        (piece,) * groups,
        gram,
        rest,
        scratch=[pltpu.VMEM((groups, 2 * own, per * LANES), jnp.float32)],
    )
    pieces = exchanged(pieces, "ba")
    (ortho,) = call(
        functools.partial(place_kernel, groups, own, blocks),
        (shape_of(own * 2 * blocks, LANES),),
        *pieces,
    )
    ortho = ortho.reshape(own * 2 * COMPS, sites // LANES, slices, LANES).swapaxes(1, 2)
    ortho = ortho.reshape(own, *search_block.shape[1:])
    return ortho, over.reshape(2, vectors, kept).swapaxes(1, 2)


def solution(mesh):
    placed = (
        P(None, None, None, None, "ta", None),
        P("ba", None, None, None, "ta", None),
        P(None, None, None, None, "ta", None),
        P(None, None, None, None, "ta", None),
    )
    return jax.shard_map(
        per_device,
        mesh=mesh,
        in_specs=placed,
        out_specs=(P("ba", None, None, None, "ta", None), P(None, "ba", None)),
        check_vma=False,
    )
```

```python
import functools

import jax
import jax.numpy as jnp
from jax import lax
from jax.experimental import pallas as pl
from jax.experimental.pallas import tpu as pltpu
from jax.sharding import PartitionSpec as P


HOPPING = 0.13
LANES = 128
COMPS = 12
PROJECT = (
    ((1, 1), (0, 1)),
    ((1, 0), (0, 2)),
    ((0, 1), (1, 3)),
    ((0, 2), (1, 2)),
)
REBUILD = (
    ((1, 3), (0, 3)),
    ((1, 0), (0, 2)),
    ((0, 3), (1, 1)),
    ((0, 2), (1, 2)),
)


def add_phase(left, right, phase):
    a, b = left
    c, d = right
    phase %= 4
    if phase == 0:
        return a + c, b + d
    if phase == 1:
        return a - d, b + c
    if phase == 2:
        return a - c, b - d
    return a + d, b - c


def plus(left, right):
    return left[0] + right[0], left[1] + right[1]


def minus(left, right):
    return left[0] - right[0], left[1] - right[1]


def rolled(value, shift, axis):
    shift %= value.shape[axis]
    return pltpu.roll(value, shift, axis) if shift else value


class Lattice:
    def __init__(self, slices, sites):
        self.slices = slices
        self.side = round(sites ** (1 / 3))
        self.rows = slices * sites // LANES
        self.shape = (self.rows, LANES)
        if self.side**3 != sites or LANES % (self.side * self.side) or COMPS % slices:
            raise ValueError("lattice shape")

    def masks(self):
        lane = lax.broadcasted_iota(jnp.int32, self.shape, 1)
        row = lax.broadcasted_iota(jnp.int32, self.shape, 0)
        side = self.side
        self.time = row % self.slices
        self.x_low = lane // (side * side)
        self.y = lane // side % side
        self.z = lane % side

    def shift(self, value, direction, ahead):
        side, area = self.side, self.side * self.side
        if direction == 0:
            step = 1 if ahead else -1
            edge = self.x_low == (0 if ahead else LANES // area - 1)
            mixed = jnp.where(edge, rolled(value, -step * self.slices, 0), value)
            return rolled(mixed, -step * area, 1)
        if direction < 3:
            place, unit = (self.y, side) if direction == 1 else (self.z, 1)
            edge = place == (side - 1 if ahead else 0)
            step = unit if ahead else -unit
            return jnp.where(
                edge, rolled(value, (side - 1) * step, 1), rolled(value, -step, 1)
            )
        if ahead:
            return jnp.where(self.time == self.slices - 1, 0.0, rolled(value, -1, 0))
        return jnp.where(self.time == 0, 0.0, rolled(value, 1, 0))


def load_spinor(ref, vector):
    def at(spin, colour):
        place = vector * (2 * COMPS) + spin * 3 + colour
        return ref[place], ref[place + COMPS]

    return at


def link_at(links, direction):
    def at(row, column):
        place = direction * 18 + row * 3 + column
        return links[place], links[place + 9]

    return at


def times_link(link, half):
    out = []
    for row in range(3):
        re = im = None
        for column in range(3):
            u, v = link(row, column)
            a, b = half[column]
            re = u * a - v * b if re is None else re + u * a - v * b
            im = u * b + v * a if im is None else im + u * b + v * a
        out.append((re, im))
    return out


def times_dagger(link, half):
    out = []
    for row in range(3):
        re = im = None
        for column in range(3):
            u, v = link(column, row)
            a, b = half[column]
            re = u * a + v * b if re is None else re + u * a + v * b
            im = u * b - v * a if im is None else im + u * b - v * a
        out.append((re, im))
    return out


def half_spinor(spinor, direction, spin, ahead):
    other, phase = PROJECT[direction][spin]
    phase = phase if ahead else phase + 2
    return [add_phase(spinor(spin, c), spinor(2 + other, c), phase) for c in range(3)]


def pack_rim(lattice, spinor, links, ahead_ref, behind_ref, vector):
    slices = lattice.slices
    ahead, behind = [], []
    for spin in range(2):
        ahead += half_spinor(spinor, 3, spin, True)
        behind += times_dagger(link_at(links, 3), half_spinor(spinor, 3, spin, False))
    for values, origin, ref in ((ahead, 0, ahead_ref), (behind, slices - 1, behind_ref)):
        flat = [part for pair in values for part in pair]
        for group in range(COMPS // slices):
            tile = None
            for place in range(slices):
                moved = rolled(flat[group * slices + place], place - origin, 0)
                tile = moved if tile is None else jnp.where(lattice.time == place, moved, tile)
            ref[vector * (COMPS // slices) + group] = tile


def unpack_rim(lattice, ref, vector, ahead, sign):
    slices = lattice.slices
    target = slices - 1 if ahead else 0
    flat = []
    for comp in range(COMPS):
        tile = ref[vector * (COMPS // slices) + comp // slices]
        moved = rolled(tile, target - comp % slices, 0)
        flat.append(jnp.where(lattice.time == target, moved * sign, 0.0))
    return [(flat[2 * i], flat[2 * i + 1]) for i in range(COMPS // 2)]


def pack_kernel(lattice, vectors, psi, links, ahead_ref, behind_ref):
    lattice.masks()

    def body(vector, carry):
        pack_rim(lattice, load_spinor(psi, vector), links, ahead_ref, behind_ref, vector)
        return carry

    lax.fori_loop(0, vectors, body, 0)


def local_kernel(lattice, vectors, psi, links, clover, out):
    lattice.masks()

    def body(vector, carry):
        spinor = load_spinor(psi, vector)
        upper = [[None] * 3 for _ in range(2)]
        lower = [[None] * 3 for _ in range(2)]
        for direction in range(4):
            link = link_at(links, direction)
            for spin in range(2):
                half = half_spinor(spinor, direction, spin, True)
                half = [tuple(lattice.shift(p, direction, True) for p in h) for h in half]
                ahead = times_link(link, half)
                half = half_spinor(spinor, direction, spin, False)
                behind = times_dagger(link, half)
                behind = [tuple(lattice.shift(p, direction, False) for p in h) for h in behind]
                place, phase = REBUILD[direction][spin]
                for c in range(3):
                    total, diff = plus(ahead[c], behind[c]), minus(ahead[c], behind[c])
                    if upper[spin][c] is None:
                        upper[spin][c] = total
                    else:
                        upper[spin][c] = plus(upper[spin][c], total)
                    if lower[place][c] is None:
                        zero = jnp.zeros_like(diff[0])
                        lower[place][c] = add_phase((zero, zero), diff, phase)
                    else:
                        lower[place][c] = add_phase(lower[place][c], diff, phase)
        for chiral, hops in ((0, upper), (1, lower)):
            for row in range(6):
                re = im = None
                for column in range(6):
                    place = chiral * 72 + row * 6 + column
                    u, v = clover[place], clover[place + 36]
                    a, b = spinor(2 * chiral + column // 3, column % 3)
                    re = u * a - v * b if re is None else re + u * a - v * b
                    im = u * b + v * a if im is None else im + u * b + v * a
                place = vector * (2 * COMPS) + chiral * 6 + row
                out[place] = re - HOPPING * hops[row // 3][row % 3][0]
                out[place + COMPS] = im - HOPPING * hops[row // 3][row % 3][1]
        return carry

    lax.fori_loop(0, vectors, body, 0)


def rim_signs():
    count, here = lax.axis_size("ta"), lax.axis_index("ta")
    one = jnp.float32(1.0)
    return jnp.where(here == count - 1, -one, one), jnp.where(here == 0, -one, one)


def finish(lattice, links, part, rim_ahead, rim_behind, vector, signs, store):
    ahead_all = unpack_rim(lattice, rim_ahead, vector, True, signs[0])
    behind_all = unpack_rim(lattice, rim_behind, vector, False, signs[1])
    for spin in range(2):
        ahead = times_link(link_at(links, 3), ahead_all[3 * spin : 3 * spin + 3])
        behind = behind_all[3 * spin : 3 * spin + 3]
        for c in range(3):
            for ri in range(2):
                f, b = ahead[c][ri], behind[c][ri]
                place = vector * (2 * COMPS) + ri * COMPS + spin * 3 + c
                store(place, part[place] - HOPPING * (f + b))
                store(place + 6, -(part[place + 6] + HOPPING * (f - b)))


def middle_kernel(
    lattice, vectors, part, links, rim_ahead, rim_behind, out, ahead_ref, behind_ref
):
    lattice.masks()
    signs = rim_signs()

    def body(vector, carry):
        def store(place, value):
            out[place] = value

        finish(lattice, links, part, rim_ahead, rim_behind, vector, signs, store)
        pack_rim(lattice, load_spinor(out, vector), links, ahead_ref, behind_ref, vector)
        return carry

    lax.fori_loop(0, vectors, body, 0)


def two_halves(value):
    high = value.astype(jnp.bfloat16)
    return high, (value - high.astype(jnp.float32)).astype(jnp.bfloat16)


def basis_kernel(groups, kept, blocks, basis, out):
    per = blocks // groups

    def body(block, carry):
        rows = jnp.concatenate(
            [
                basis[pl.ds(block, kept, stride=2 * blocks), :],
                basis[pl.ds(blocks + block, kept, stride=2 * blocks), :],
            ],
            axis=0,
        )
        high, low = two_halves(rows)
        lanes = pl.ds(pl.multiple_of(block % per * LANES, LANES), LANES)
        out[block // per, : 2 * kept, lanes] = high
        out[block // per, 2 * kept :, lanes] = low
        return carry

    lax.fori_loop(0, blocks, body, 0, unroll=2)


def correlate_kernel(
    lattice, groups, vectors, kept, blocks, scale,
    part, links, rim_ahead, rim_behind, basis, applied, over, field,
):
    lattice.masks()
    signs = rim_signs()
    rows = lattice.rows

    def body(vector, carry):
        def store(place, value):
            start = place * rows
            field[pl.ds(start if isinstance(start, int) else pl.multiple_of(start, rows), rows), :] = value

        finish(lattice, links, part, rim_ahead, rim_behind, vector, signs, store)
        return carry

    lax.fori_loop(0, vectors, body, 0)
    per = blocks // groups

    def relay(block, carry):
        lanes = pl.ds(pl.multiple_of(block % per * LANES, LANES), LANES)
        for ri in range(2):
            start = ri * blocks + block
            applied[block // per, ri * vectors : (ri + 1) * vectors, lanes] = field[
                pl.ds(start, vectors, stride=2 * blocks), :
            ]
        return carry

    lax.fori_loop(0, blocks, relay, 0, unroll=2)
    total = None
    for group in range(groups):
        both = jnp.concatenate(two_halves(applied[group]), axis=0)
        term = lax.dot_general(
            both, basis[group], (((1,), (1,)), ((), ())), preferred_element_type=jnp.float32
        )
        total = term if total is None else total + term
    total = total[: 2 * vectors] + total[2 * vectors :]
    total = total[:, : 2 * kept] + total[:, 2 * kept :]
    real, imag = total[:vectors], total[vectors:]
    over[:vectors, :] = scale * (real[:, :kept] + imag[:, kept:])
    over[vectors:, :] = scale * (imag[:, :kept] - real[:, kept:])


def partner(here, step, count):
    if count & (count - 1) == 0:
        return here ^ step
    return (here + step) % count


def source(here, step, count):
    if count & (count - 1) == 0:
        return here ^ step
    return (here + count - step) % count


def exchanged(values, axis):
    count = lax.axis_size(axis)
    out = [values[0]]
    for step in range(1, count):
        pairs = [(i, partner(i, step, count)) for i in range(count)]
        out.append(lax.ppermute(values[step], axis, pairs))
    return out


def summed(value, axis):
    count = lax.axis_size(axis)
    if count & (count - 1):
        return lax.psum(value, axis)
    step = 1
    while step < count:
        value = value + lax.ppermute(value, axis, [(i, i ^ step) for i in range(count)])
        step *= 2
    return value


def weight_rows(real, imag):
    weight = jnp.concatenate(
        [jnp.concatenate([real, -imag], axis=1), jnp.concatenate([imag, real], axis=1)], axis=0
    )
    high, low = two_halves(weight)
    return jnp.concatenate(
        [jnp.concatenate([high, high], axis=1), jnp.concatenate([low, low], axis=1)], axis=0
    )


def weighted(weight, basis):
    both = jnp.dot(weight, basis, preferred_element_type=jnp.float32)
    half = both.shape[0] // 2
    return both[:half] + both[half:]


def slice_kernel(groups, rows, ship, basis, *outs):
    here = lax.axis_index("ba")
    per = basis.shape[1] // groups
    for step in range(1, groups):
        start = pl.multiple_of(partner(here, step, groups) * per, rows)
        outs[step - 1][...] = basis[:, pl.ds(start, ship), :]


def relay_kernel(kept, blocks, *refs):
    count = len(refs) // 2
    for part, out in zip(refs[:count], refs[count:]):

        def body(block, carry, part=part, out=out):
            lanes = pl.ds(pl.multiple_of(block * LANES, LANES), LANES)
            for ri in range(2):
                high, low = two_halves(part[pl.ds(ri * blocks + block, kept, stride=2 * blocks), :])
                out[ri * kept : (ri + 1) * kept, lanes] = high
                out[(2 + ri) * kept : (3 + ri) * kept, lanes] = low
            return carry

        lax.fori_loop(0, blocks, body, 0, unroll=2)


def project_kernel(groups, vectors, kept, shipped, over, basis, *outs):
    here = lax.axis_index("ba")
    weight = weight_rows(over[:vectors, :], over[vectors:, :])
    for step in range(groups):
        other = partner(here, step, groups)
        value = weighted(weight, basis[other, :, shipped:])
        width = value.shape[1]
        outs[step][:, :width] = value
        outs[step][:, width:] = jnp.zeros((2 * vectors, LANES), jnp.float32)
        outs[step][:, width : width + kept] = over[...]


def rest_kernel(groups, vectors, kept, shipped, scale, over, basis, applied, *refs):
    parts, refs = refs[:groups], refs[groups:]
    pieces, (rest_ref, gram) = refs[:-2], refs[-2:]
    here = lax.axis_index("ba")
    width = parts[0].shape[1] - LANES
    total = parts[0][:, :width]
    for part in parts[1:]:
        total = total + part[:, :width]
    if shipped:
        head = weighted(
            weight_rows(over[:vectors, :], over[vectors:, :]), basis[here, :, :shipped]
        )
        for part, piece in zip(parts[1:], pieces):
            there = part[:, width : width + kept]
            head = head + weighted(weight_rows(there[:vectors], there[vectors:]), piece[...])
        total = jnp.concatenate([head, total], axis=1)
    rest = applied[here] - total
    rest_ref[...] = rest
    both = jnp.concatenate(two_halves(rest), axis=0)
    full = lax.dot_general(
        both, both, (((1,), (1,)), ((), ())), preferred_element_type=jnp.float32
    )
    full = full[: 2 * vectors] + full[2 * vectors :]
    full = full[:, : 2 * vectors] + full[:, 2 * vectors :]
    real, imag = full[:vectors], full[vectors:]
    gram[:, :vectors] = scale * (real[:, :vectors] + imag[:, vectors:])
    gram[:, vectors:] = scale * (real[:, vectors:] - imag[:, :vectors])


def ortho_kernel(groups, vectors, gram, rest, *outs):
    here = lax.axis_index("ba")
    work = outs[-1]
    outs = outs[:-1]
    shape = (vectors, 2 * vectors)
    row = lax.broadcasted_iota(jnp.int32, shape, 0)
    lane = lax.broadcasted_iota(jnp.int32, shape, 1)
    unit = jnp.where(lane == row + vectors, 1.0, 0.0)
    re = jnp.where(lane < vectors, gram[...], unit)
    im = jnp.concatenate([gram[:, vectors:], jnp.zeros((vectors, vectors), jnp.float32)], axis=1)
    for pivot in range(vectors):
        scale = 1.0 / jnp.sqrt(re[pivot : pivot + 1, pivot : pivot + 1])
        row_re, row_im = re[pivot : pivot + 1] * scale, im[pivot : pivot + 1] * scale
        col_re, col_im = re[:, pivot : pivot + 1] * scale, im[:, pivot : pivot + 1] * scale
        below = row > pivot
        new_re = re - (col_re * row_re - col_im * row_im)
        new_im = im - (col_re * row_im + col_im * row_re)
        re = jnp.where(below, new_re, jnp.where(row == pivot, row_re, re))
        im = jnp.where(below, new_im, jnp.where(row == pivot, row_im, im))
    inv_re, inv_im = re[:, vectors:], im[:, vectors:]
    weight = weight_rows(inv_re, -inv_im)
    both = jnp.concatenate(two_halves(rest[...]), axis=0)
    full = weighted(weight, both)
    own = vectors // groups
    for group in range(groups):
        for ri in range(2):
            start = ri * vectors + group * own
            work[group, ri * own : (ri + 1) * own, :] = full[start : start + own]
    for step in range(groups):
        outs[step][...] = work[partner(here, step, groups)]


def place_kernel(groups, own, blocks, *refs):
    parts, out = refs[:groups], refs[groups]
    here = lax.axis_index("ba")
    per = blocks // groups
    for step in range(groups):
        first = source(here, step, groups) * per
        for block in range(per):
            for ri in range(2):
                value = parts[step][ri * own : (ri + 1) * own, block * LANES : (block + 1) * LANES]
                out[pl.ds(first + block + ri * blocks, own, stride=2 * blocks), :] = value


def call(kernel, outs, *args, scratch=(), flops=0, grant=6):
    nbytes = sum(a.size * a.dtype.itemsize for a in (*args, *outs))
    spec = pl.BlockSpec(memory_space=pltpu.VMEM)
    return pl.pallas_call(
        kernel,
        out_shape=tuple(outs),
        in_specs=[spec] * len(args),
        out_specs=tuple([spec] * len(outs)),
        scratch_shapes=list(scratch),
        compiler_params=pltpu.CompilerParams(vmem_limit_bytes=grant << 20),
        cost_estimate=pl.CostEstimate(flops=flops, bytes_accessed=nbytes, transcendentals=0),
    )(*args)


def shape_of(*dims):
    return jax.ShapeDtypeStruct(dims, jnp.float32)


def tiles_of(value, leading):
    slices, sites = value.shape[-2:]
    value = value.reshape(leading, slices, sites // LANES, LANES)
    return value.swapaxes(1, 2).reshape(leading, slices * sites // LANES, LANES)


def per_device(search_block, kept_basis, gauge_links, clover_term):
    vectors, kept = search_block.shape[0], kept_basis.shape[0]
    slices, sites = search_block.shape[-2:]
    groups, places = lax.axis_size("ba"), lax.axis_size("ta")
    lattice = Lattice(slices, sites)
    rows = lattice.rows
    blocks = COMPS * rows
    per = blocks // groups
    own = vectors // groups
    scale = 1.0 / (2 * COMPS * slices * sites * places)
    psi = tiles_of(search_block, vectors * 2 * COMPS)
    basis = tiles_of(kept_basis, kept * 2 * COMPS).reshape(kept * 2 * blocks, LANES)
    ahead_comps = 2 * (COMPS // groups) // 3 if COMPS % groups == 0 else 0
    ship = ahead_comps * rows
    shipped = ship * LANES
    links = tiles_of(gauge_links, 72)
    clover = tiles_of(clover_term, 144)
    rim = shape_of(vectors * COMPS // slices, rows, LANES)
    field = shape_of(vectors * 2 * COMPS, rows, LANES)
    work = vectors * rows * LANES

    def swap(ahead, behind):
        down = [(i, (i + places - 1) % places) for i in range(places)]
        up = [(i, (i + 1) % places) for i in range(places)]
        return lax.ppermute(ahead, "ta", down), lax.ppermute(behind, "ta", up)

    ahead, behind = call(
        functools.partial(pack_kernel, lattice, vectors), (rim, rim), psi, links, flops=200 * work
    )
    rims = swap(ahead, behind)
    pieces = []
    if ship:
        pieces = call(
            functools.partial(slice_kernel, groups, rows, ship),
            (shape_of(2 * kept, ship, LANES),) * (groups - 1),
            basis.reshape(2 * kept, blocks, LANES),
        )
        pieces = exchanged([None, *pieces], "ba")[1:]
    local = functools.partial(local_kernel, lattice, vectors)
    (part,) = call(local, (field,), psi, links, clover, flops=2000 * work)
    (rows_of_basis,) = call(
        functools.partial(basis_kernel, groups, kept, blocks),
        (jax.ShapeDtypeStruct((groups, 4 * kept, per * LANES), jnp.bfloat16),),
        basis,
    )
    first, ahead, behind = call(
        functools.partial(middle_kernel, lattice, vectors),
        (field, rim, rim),
        part,
        links,
        *rims,
        flops=400 * work,
    )
    rims = swap(ahead, behind)
    (part,) = call(local, (field,), first, links, clover, flops=2000 * work)
    applied, over = call(
        functools.partial(correlate_kernel, lattice, groups, vectors, kept, blocks, scale),
        (shape_of(groups, 2 * vectors, per * LANES), shape_of(2 * vectors, kept)),
        part,
        links,
        *rims,
        rows_of_basis,
        scratch=[pltpu.VMEM((vectors * 2 * blocks, LANES), jnp.float32)],
        flops=400 * work,
    )
    over = summed(over, "ta")
    parts = call(
        functools.partial(project_kernel, groups, vectors, kept, shipped),
        (shape_of(2 * vectors, (per + 1) * LANES - shipped),) * groups,
        over,
        rows_of_basis,
    )
    parts = exchanged(parts, "ba")
    if ship:
        pieces = call(
            functools.partial(relay_kernel, kept, ship),
            (jax.ShapeDtypeStruct((4 * kept, shipped), jnp.bfloat16),) * (groups - 1),
            *(piece.reshape(2 * kept * ship, LANES) for piece in pieces),
        )
    rest, gram = call(
        functools.partial(rest_kernel, groups, vectors, kept, shipped, scale),
        (shape_of(2 * vectors, per * LANES), shape_of(vectors, 2 * vectors)),
        over,
        rows_of_basis,
        applied,
        *parts,
        *pieces,
    )
    gram = summed(summed(gram, "ta"), "ba")
    piece = shape_of(2 * own, per * LANES)
    pieces = call(
        functools.partial(ortho_kernel, groups, vectors),
        (piece,) * groups,
        gram,
        rest,
        scratch=[pltpu.VMEM((groups, 2 * own, per * LANES), jnp.float32)],
    )
    pieces = exchanged(pieces, "ba")
    (ortho,) = call(
        functools.partial(place_kernel, groups, own, blocks),
        (shape_of(own * 2 * blocks, LANES),),
        *pieces,
    )
    ortho = ortho.reshape(own * 2 * COMPS, sites // LANES, slices, LANES).swapaxes(1, 2)
    ortho = ortho.reshape(own, *search_block.shape[1:])
    return ortho, over.reshape(2, vectors, kept).swapaxes(1, 2)


def solution(mesh):
    placed = (
        P(None, None, None, None, "ta", None),
        P("ba", None, None, None, "ta", None),
        P(None, None, None, None, "ta", None),
        P(None, None, None, None, "ta", None),
    )

    return jax.shard_map(
        per_device,
        mesh=mesh,
        in_specs=placed,
        out_specs=(P("ba", None, None, None, "ta", None), P(None, "ba", None)),
        check_vma=False,
    )
```

```python
import functools

import jax
import jax.numpy as jnp
from jax import lax
from jax.experimental import pallas as pl
from jax.experimental.pallas import tpu as pltpu
from jax.sharding import PartitionSpec as P


HOPPING = 0.13
LANES = 128
COMPS = 12
PROJECT = (
    ((1, 1), (0, 1)),
    ((1, 0), (0, 2)),
    ((0, 1), (1, 3)),
    ((0, 2), (1, 2)),
)
REBUILD = (
    ((1, 3), (0, 3)),
    ((1, 0), (0, 2)),
    ((0, 3), (1, 1)),
    ((0, 2), (1, 2)),
)


def add_phase(left, right, phase):
    a, b = left
    c, d = right
    phase %= 4
    if phase == 0:
        return a + c, b + d
    if phase == 1:
        return a - d, b + c
    if phase == 2:
        return a - c, b - d
    return a + d, b - c


def plus(left, right):
    return left[0] + right[0], left[1] + right[1]


def minus(left, right):
    return left[0] - right[0], left[1] - right[1]


def rolled(value, shift, axis):
    shift %= value.shape[axis]
    return pltpu.roll(value, shift, axis) if shift else value


class Lattice:
    def __init__(self, slices, sites):
        self.slices = slices
        self.side = round(sites ** (1 / 3))
        self.rows = slices * sites // LANES
        self.shape = (self.rows, LANES)
        if self.side**3 != sites or LANES % (self.side * self.side) or COMPS % slices:
            raise ValueError("lattice shape")

    def masks(self):
        lane = lax.broadcasted_iota(jnp.int32, self.shape, 1)
        row = lax.broadcasted_iota(jnp.int32, self.shape, 0)
        side = self.side
        self.time = row % self.slices
        self.x_low = lane // (side * side)
        self.y = lane // side % side
        self.z = lane % side

    def shift(self, value, direction, ahead):
        side, area = self.side, self.side * self.side
        if direction == 0:
            step = 1 if ahead else -1
            edge = self.x_low == (0 if ahead else LANES // area - 1)
            mixed = jnp.where(edge, rolled(value, -step * self.slices, 0), value)
            return rolled(mixed, -step * area, 1)
        if direction < 3:
            place, unit = (self.y, side) if direction == 1 else (self.z, 1)
            edge = place == (side - 1 if ahead else 0)
            step = unit if ahead else -unit
            return jnp.where(
                edge, rolled(value, (side - 1) * step, 1), rolled(value, -step, 1)
            )
        if ahead:
            return jnp.where(self.time == self.slices - 1, 0.0, rolled(value, -1, 0))
        return jnp.where(self.time == 0, 0.0, rolled(value, 1, 0))


def load_spinor(ref, vector):
    def at(spin, colour):
        place = vector * (2 * COMPS) + spin * 3 + colour
        return ref[place], ref[place + COMPS]

    return at


def link_at(links, direction):
    def at(row, column):
        place = direction * 18 + row * 3 + column
        return links[place], links[place + 9]

    return at


def times_link(link, half):
    out = []
    for row in range(3):
        re = im = None
        for column in range(3):
            u, v = link(row, column)
            a, b = half[column]
            re = u * a - v * b if re is None else re + u * a - v * b
            im = u * b + v * a if im is None else im + u * b + v * a
        out.append((re, im))
    return out


def times_dagger(link, half):
    out = []
    for row in range(3):
        re = im = None
        for column in range(3):
            u, v = link(column, row)
            a, b = half[column]
            re = u * a + v * b if re is None else re + u * a + v * b
            im = u * b - v * a if im is None else im + u * b - v * a
        out.append((re, im))
    return out


def half_spinor(spinor, direction, spin, ahead):
    other, phase = PROJECT[direction][spin]
    phase = phase if ahead else phase + 2
    return [add_phase(spinor(spin, c), spinor(2 + other, c), phase) for c in range(3)]


def pack_rim(lattice, spinor, links, direction, ahead_ref, behind_ref, vector):
    slices = lattice.slices
    ahead, behind = [], []
    for spin in range(2):
        ahead += half_spinor(spinor, 3, spin, True)
        behind += times_dagger(link_at(links, direction), half_spinor(spinor, 3, spin, False))
    for values, origin, ref in ((ahead, 0, ahead_ref), (behind, slices - 1, behind_ref)):
        flat = [part for pair in values for part in pair]
        for group in range(COMPS // slices):
            tile = None
            for place in range(slices):
                moved = rolled(flat[group * slices + place], place - origin, 0)
                tile = moved if tile is None else jnp.where(lattice.time == place, moved, tile)
            ref[vector * (COMPS // slices) + group] = tile


def unpack_rim(lattice, ref, vector, ahead, sign):
    slices = lattice.slices
    target = slices - 1 if ahead else 0
    flat = []
    for comp in range(COMPS):
        tile = ref[vector * (COMPS // slices) + comp // slices]
        moved = rolled(tile, target - comp % slices, 0)
        flat.append(jnp.where(lattice.time == target, moved * sign, 0.0))
    return [(flat[2 * i], flat[2 * i + 1]) for i in range(COMPS // 2)]


def open_kernel(
    lattice, groups, vectors, kept, ship,
    psi_ref, links_ref, basis, ahead_ref, behind_ref, *refs,
):
    pieces = refs[: groups - 1]
    psi, links, held, sems = refs[groups - 1 :]
    here = lax.axis_index("ba")
    rows, per = lattice.rows, basis.shape[2] // groups
    count = links.shape[0]
    fields = pltpu.make_async_copy(psi_ref, psi, sems.at[0])
    links_in = pltpu.make_async_copy(links_ref.at[pl.ds(3 * count, count)], links, sems.at[1])
    kept_in = []
    for step in range(1, groups if ship else 1):
        start = pl.multiple_of(partner(here, step, groups) * per, rows)
        kept_in.append(
            pltpu.make_async_copy(
                basis.at[:, :, pl.ds(start, held.shape[3]), :], held.at[step - 1], sems.at[1 + step]
            )
        )
    for copy in (links_in, fields, *kept_in):
        copy.start()
    lattice.masks()
    links_in.wait()
    fields.wait()

    def body(vector, carry):
        pack_rim(lattice, load_spinor(psi, vector), links, 0, ahead_ref, behind_ref, vector)
        return carry

    lax.fori_loop(0, vectors, body, 0)
    for step, copy in enumerate(kept_in):
        copy.wait()

        def turn(group, carry, step=step):
            first = pl.multiple_of(group * 8, 8)
            for ri in range(2):
                for start in range(0, ship, rows):
                    tile = held[step, pl.ds(first, 8), ri, start : start + rows, :]
                    tile = jnp.swapaxes(tile, 0, 1)
                    size = min(rows, ship - start)
                    pieces[step][start : start + size, pl.ds(ri * kept + first, 8), :] = tile[:size]
            return carry

        lax.fori_loop(0, kept // 8, turn, 0)


def basis_kernel(rows, kept, basis, out):
    def body(tile, carry):
        blocks = pl.ds(pl.multiple_of(tile * rows, rows), rows)
        for ri in range(2):
            for first in range(0, kept, 16):
                value = jnp.swapaxes(basis[first : first + 16, ri, blocks, :], 0, 1)
                high, low = two_halves(value)
                start = ri * kept + first
                out[blocks, start : start + 16, :] = high
                out[blocks, 2 * kept + start : 2 * kept + start + 16, :] = low
        return carry

    lax.fori_loop(0, basis.shape[2] // rows, body, 0)


def local_kernel(lattice, vectors, psi, links, clover, out):
    lattice.masks()

    def body(vector, carry):
        spinor = load_spinor(psi, vector)
        upper = [[None] * 3 for _ in range(2)]
        lower = [[None] * 3 for _ in range(2)]
        for direction in range(4):
            link = link_at(links, direction)
            for spin in range(2):
                half = half_spinor(spinor, direction, spin, True)
                half = [tuple(lattice.shift(p, direction, True) for p in h) for h in half]
                ahead = times_link(link, half)
                half = half_spinor(spinor, direction, spin, False)
                behind = times_dagger(link, half)
                behind = [tuple(lattice.shift(p, direction, False) for p in h) for h in behind]
                place, phase = REBUILD[direction][spin]
                for c in range(3):
                    total, diff = plus(ahead[c], behind[c]), minus(ahead[c], behind[c])
                    if upper[spin][c] is None:
                        upper[spin][c] = total
                    else:
                        upper[spin][c] = plus(upper[spin][c], total)
                    if lower[place][c] is None:
                        zero = jnp.zeros_like(diff[0])
                        lower[place][c] = add_phase((zero, zero), diff, phase)
                    else:
                        lower[place][c] = add_phase(lower[place][c], diff, phase)
        for chiral, hops in ((0, upper), (1, lower)):
            for row in range(6):
                re = im = None
                for column in range(6):
                    place = chiral * 72 + row * 6 + column
                    u, v = clover[place], clover[place + 36]
                    a, b = spinor(2 * chiral + column // 3, column % 3)
                    re = u * a - v * b if re is None else re + u * a - v * b
                    im = u * b + v * a if im is None else im + u * b + v * a
                place = vector * (2 * COMPS) + chiral * 6 + row
                out[place] = re - HOPPING * hops[row // 3][row % 3][0]
                out[place + COMPS] = im - HOPPING * hops[row // 3][row % 3][1]
        return carry

    lax.fori_loop(0, vectors, body, 0)


def rim_signs():
    count, here = lax.axis_size("ta"), lax.axis_index("ta")
    one = jnp.float32(1.0)
    return jnp.where(here == count - 1, -one, one), jnp.where(here == 0, -one, one)


def finish(lattice, links, part, rim_ahead, rim_behind, vector, signs, store):
    ahead_all = unpack_rim(lattice, rim_ahead, vector, True, signs[0])
    behind_all = unpack_rim(lattice, rim_behind, vector, False, signs[1])
    for spin in range(2):
        ahead = times_link(link_at(links, 3), ahead_all[3 * spin : 3 * spin + 3])
        behind = behind_all[3 * spin : 3 * spin + 3]
        for c in range(3):
            for ri in range(2):
                f, b = ahead[c][ri], behind[c][ri]
                place = vector * (2 * COMPS) + ri * COMPS + spin * 3 + c
                store(place, part[place] - HOPPING * (f + b))
                store(place + 6, -(part[place + 6] + HOPPING * (f - b)))


def middle_kernel(
    lattice, vectors, part, links, rim_ahead, rim_behind, out, ahead_ref, behind_ref
):
    lattice.masks()
    signs = rim_signs()

    def body(vector, carry):
        def store(place, value):
            out[place] = value

        finish(lattice, links, part, rim_ahead, rim_behind, vector, signs, store)
        pack_rim(lattice, load_spinor(out, vector), links, 3, ahead_ref, behind_ref, vector)
        return carry

    lax.fori_loop(0, vectors, body, 0)


def two_halves(value):
    high = value.astype(jnp.bfloat16)
    return high, (value - high.astype(jnp.float32)).astype(jnp.bfloat16)


def pair_of(ref, block):
    return jnp.concatenate([ref[block], ref[block + 1]], axis=1)


def row_pairs(ref, block):
    return jnp.concatenate(two_halves(pair_of(ref, block)), axis=0)


def correlate_kernel(
    lattice, vectors, kept, scale,
    part, links, rim_ahead, rim_behind, basis, applied, over, field,
):
    lattice.masks()
    signs = rim_signs()
    rows = lattice.rows

    def body(vector, carry):
        def store(place, value):
            field[place] = value

        finish(lattice, links, part, rim_ahead, rim_behind, vector, signs, store)
        return carry

    lax.fori_loop(0, vectors, body, 0)

    def add(comp, total):
        blocks_here = pl.ds(pl.multiple_of(comp * rows, rows), rows)
        for ri in range(2):
            for first in range(0, vectors, 8):
                tiles = jnp.stack(
                    [field[(first + i) * 2 * COMPS + ri * COMPS + comp] for i in range(8)]
                )
                start = ri * vectors + first
                applied[blocks_here, start : start + 8, :] = jnp.swapaxes(tiles, 0, 1)
        for place in range(0, rows, 2):
            block = comp * rows + place
            total = total + lax.dot_general(
                row_pairs(applied, block),
                pair_of(basis, block),
                (((1,), (1,)), ((), ())),
                preferred_element_type=jnp.float32,
            )
        return total

    total = lax.fori_loop(0, COMPS, add, jnp.zeros((4 * vectors, 4 * kept), jnp.float32))
    total = total[: 2 * vectors] + total[2 * vectors :]
    total = total[:, : 2 * kept] + total[:, 2 * kept :]
    real, imag = total[:vectors], total[vectors:]
    over[:vectors, :] = scale * (real[:, :kept] + imag[:, kept:])
    over[vectors:, :] = scale * (imag[:, :kept] - real[:, kept:])


def partner(here, step, count):
    if count & (count - 1) == 0:
        return here ^ step
    return (here + step) % count


def source(here, step, count):
    if count & (count - 1) == 0:
        return here ^ step
    return (here + count - step) % count


def exchanged(values, axis):
    count = lax.axis_size(axis)
    out = [values[0]]
    for step in range(1, count):
        pairs = [(i, partner(i, step, count)) for i in range(count)]
        out.append(lax.ppermute(values[step], axis, pairs))
    return out


def summed(value, axis, radix):
    count = lax.axis_size(axis)
    if count & (count - 1):
        return lax.psum(value, axis)
    stride = 1
    while stride < count:
        size, radix = min(radix[0], count // stride), radix[1:] or radix
        total = value
        for step in range(1, size):
            total = total + lax.ppermute(
                value, axis, [(i, i ^ (step * stride)) for i in range(count)]
            )
        value = total
        stride *= size
    return value


def weight_rows(real, imag):
    weight = jnp.concatenate(
        [jnp.concatenate([real, -imag], axis=1), jnp.concatenate([imag, real], axis=1)], axis=0
    )
    high, low = two_halves(weight)
    return jnp.concatenate(
        [jnp.concatenate([high, high], axis=1), jnp.concatenate([low, low], axis=1)], axis=0
    )


def weighted(weight, basis):
    both = jnp.dot(weight, basis, preferred_element_type=jnp.float32)
    half = both.shape[0] // 2
    return both[:half] + both[half:]


def project_kernel(groups, vectors, kept, ship, over, basis, *outs):
    here = lax.axis_index("ba")
    per = basis.shape[0] // groups
    weight = weight_rows(over[:vectors, :], over[vectors:, :])
    for step in range(groups):
        first = partner(here, step, groups) * per + ship
        for block in range(0, per - ship, 2):
            value = weighted(weight, pair_of(basis, first + block))
            outs[step][block] = value[:, :LANES]
            outs[step][block + 1] = value[:, LANES:]
        outs[step][per - ship] = jnp.zeros((2 * vectors, LANES), jnp.float32)
        outs[step][per - ship, :, :kept] = over[...]


def rest_kernel(groups, vectors, kept, ship, scale, over, basis, applied, *refs):
    parts, refs = refs[:groups], refs[groups:]
    pieces, (rest_ref, gram) = refs[:-2], refs[-2:]
    here = lax.axis_index("ba")
    per = basis.shape[0] // groups
    weights = [weight_rows(over[:vectors, :], over[vectors:, :])]
    for part in parts[1:]:
        there = part[per - ship, :, :kept]
        weights.append(weight_rows(there[:vectors], there[vectors:]))
    full = None
    for block in range(0, per, 2):
        mine = here * per + block
        if block < ship:
            total = weighted(weights[0], pair_of(basis, mine))
            for weight, piece in zip(weights[1:], pieces):
                total = total + weighted(weight, row_pairs(piece, block))
        else:
            total = [
                sum((part[block + i - ship] for part in parts[1:]), parts[0][block + i - ship])
                for i in range(2)
            ]
            total = jnp.concatenate(total, axis=1)
        rest = pair_of(applied, mine) - total
        rest_ref[block] = rest[:, :LANES]
        rest_ref[block + 1] = rest[:, LANES:]
        both = jnp.concatenate(two_halves(rest), axis=0)
        term = lax.dot_general(
            both, both, (((1,), (1,)), ((), ())), preferred_element_type=jnp.float32
        )
        full = term if full is None else full + term
    full = full[: 2 * vectors] + full[2 * vectors :]
    full = full[:, : 2 * vectors] + full[:, 2 * vectors :]
    real, imag = full[:vectors], full[vectors:]
    gram[:, :vectors] = scale * (real[:, :vectors] + imag[:, vectors:])
    gram[:, vectors:] = scale * (real[:, vectors:] - imag[:, :vectors])


def ortho_kernel(groups, vectors, gram, rest, *outs):
    here = lax.axis_index("ba")
    work = outs[-1]
    outs = outs[:-1]
    shape = (vectors, 2 * vectors)
    row = lax.broadcasted_iota(jnp.int32, shape, 0)
    lane = lax.broadcasted_iota(jnp.int32, shape, 1)
    unit = jnp.where(lane == row + vectors, 1.0, 0.0)
    re = jnp.where(lane < vectors, gram[...], unit)
    im = jnp.concatenate([gram[:, vectors:], jnp.zeros((vectors, vectors), jnp.float32)], axis=1)
    for pivot in range(vectors):
        scale = 1.0 / jnp.sqrt(re[pivot : pivot + 1, pivot : pivot + 1])
        row_re, row_im = re[pivot : pivot + 1] * scale, im[pivot : pivot + 1] * scale
        col_re, col_im = re[:, pivot : pivot + 1] * scale, im[:, pivot : pivot + 1] * scale
        below = row > pivot
        new_re = re - (col_re * row_re - col_im * row_im)
        new_im = im - (col_re * row_im + col_im * row_re)
        re = jnp.where(below, new_re, jnp.where(row == pivot, row_re, re))
        im = jnp.where(below, new_im, jnp.where(row == pivot, row_im, im))
    inv_re, inv_im = re[:, vectors:], im[:, vectors:]
    weight = weight_rows(inv_re, -inv_im)
    own = vectors // groups
    for block in range(0, rest.shape[0], 2):
        full = weighted(weight, row_pairs(rest, block))
        for i in range(2):
            value = full[:, i * LANES : (i + 1) * LANES]
            for group in range(groups):
                for ri in range(2):
                    start = ri * vectors + group * own
                    work[group, block + i, ri * own : (ri + 1) * own, :] = value[
                        start : start + own
                    ]
    for step in range(groups):
        outs[step][...] = work[partner(here, step, groups)]


def place_kernel(groups, own, blocks, *refs):
    parts, out = refs[:groups], refs[groups]
    here = lax.axis_index("ba")
    per = blocks // groups
    for step in range(groups):
        first = source(here, step, groups) * per
        for block in range(per):
            for ri in range(2):
                value = parts[step][block, ri * own : (ri + 1) * own, :]
                out[pl.ds(first + block + ri * blocks, own, stride=2 * blocks), :] = value


def call(kernel, outs, *args, scratch=(), flops=0, grant=6, remote=()):
    nbytes = sum(a.size * a.dtype.itemsize for a in (*args, *outs))
    spec = pl.BlockSpec(memory_space=pltpu.VMEM)
    anywhere = pl.BlockSpec(memory_space=pltpu.HBM)
    return pl.pallas_call(
        kernel,
        out_shape=tuple(outs),
        in_specs=[anywhere if i in remote else spec for i in range(len(args))],
        out_specs=tuple([spec] * len(outs)),
        scratch_shapes=list(scratch),
        compiler_params=pltpu.CompilerParams(vmem_limit_bytes=grant << 20),
        cost_estimate=pl.CostEstimate(flops=flops, bytes_accessed=nbytes, transcendentals=0),
    )(*args)


def shape_of(*dims):
    return jax.ShapeDtypeStruct(dims, jnp.float32)


def tiles_of(value, leading):
    slices, sites = value.shape[-2:]
    value = value.reshape(leading, slices, sites // LANES, LANES)
    return value.swapaxes(1, 2).reshape(leading, slices * sites // LANES, LANES)


def per_device(search_block, kept_basis, gauge_links, clover_term):
    vectors, kept = search_block.shape[0], kept_basis.shape[0]
    slices, sites = search_block.shape[-2:]
    groups, places = lax.axis_size("ba"), lax.axis_size("ta")
    lattice = Lattice(slices, sites)
    rows = lattice.rows
    blocks = COMPS * rows
    per = blocks // groups
    own = vectors // groups
    scale = 1.0 / (2 * COMPS * slices * sites * places)
    psi = tiles_of(search_block, vectors * 2 * COMPS)
    basis = tiles_of(kept_basis, kept * 2 * COMPS).reshape(kept, 2, blocks, LANES)
    ship = per // 2 if per % rows == 0 else 0
    links = tiles_of(gauge_links, 72)
    clover = tiles_of(clover_term, 144)
    local = functools.partial(local_kernel, lattice, vectors)
    rim = shape_of(vectors * COMPS // slices, rows, LANES)
    field = shape_of(vectors * 2 * COMPS, rows, LANES)
    work = vectors * rows * LANES

    def swap(ahead, behind):
        down = [(i, (i + places - 1) % places) for i in range(places)]
        up = [(i, (i + 1) % places) for i in range(places)]
        return lax.ppermute(ahead, "ta", down), lax.ppermute(behind, "ta", up)

    ahead, behind, *pieces = call(
        functools.partial(open_kernel, lattice, groups, vectors, kept, ship),
        (rim, rim) + (shape_of(max(ship, 1), 2 * kept, LANES),) * (groups - 1),
        psi,
        links,
        basis,
        scratch=[
            pltpu.VMEM(psi.shape, jnp.float32),
            pltpu.VMEM((18, rows, LANES), jnp.float32),
            pltpu.VMEM((groups - 1, kept, 2, -(-ship // rows) * rows or rows, LANES), jnp.float32),
            pltpu.SemaphoreType.DMA((groups + 1,)),
        ],
        flops=200 * work,
        grant=60,
        remote=(0, 1, 2),
    )
    rims = swap(ahead, behind)
    if ship:
        pieces = exchanged([None, *pieces], "ba")[1:]
    else:
        pieces = []
    (part,) = call(local, (field,), psi, links, clover, flops=2000 * work)
    first, ahead, behind = call(
        functools.partial(middle_kernel, lattice, vectors),
        (field, rim, rim),
        part,
        links,
        *rims,
        flops=400 * work,
    )
    rims = swap(ahead, behind)
    (part,) = call(local, (field,), first, links, clover, flops=2000 * work)
    (basis_rows,) = call(
        functools.partial(basis_kernel, rows, kept),
        (jax.ShapeDtypeStruct((blocks, 4 * kept, LANES), jnp.bfloat16),),
        basis,
    )
    applied, over = call(
        functools.partial(correlate_kernel, lattice, vectors, kept, scale),
        (shape_of(blocks, 2 * vectors, LANES), shape_of(2 * vectors, kept)),
        part,
        links,
        *rims,
        basis_rows,
        scratch=[pltpu.VMEM(psi.shape, jnp.float32)],
        flops=400 * work,
    )
    over = summed(over, "ta", (2, 4))
    parts = call(
        functools.partial(project_kernel, groups, vectors, kept, ship),
        (shape_of(per - ship + 1, 2 * vectors, LANES),) * groups,
        over,
        basis_rows,
    )
    parts = exchanged(parts, "ba")
    rest, gram = call(
        functools.partial(rest_kernel, groups, vectors, kept, ship, scale),
        (shape_of(per, 2 * vectors, LANES), shape_of(vectors, 2 * vectors)),
        over,
        basis_rows,
        applied,
        *parts,
        *pieces,
    )
    gram = summed(summed(gram, "ta", (2, 4)), "ba", (4,))
    piece = shape_of(per, 2 * own, LANES)
    pieces = call(
        functools.partial(ortho_kernel, groups, vectors),
        (piece,) * groups,
        gram,
        rest,
        scratch=[pltpu.VMEM((groups, per, 2 * own, LANES), jnp.float32)],
    )
    pieces = exchanged(pieces, "ba")
    (ortho,) = call(
        functools.partial(place_kernel, groups, own, blocks),
        (shape_of(own * 2 * blocks, LANES),),
        *pieces,
    )
    ortho = ortho.reshape(own * 2 * COMPS, sites // LANES, slices, LANES).swapaxes(1, 2)
    ortho = ortho.reshape(own, *search_block.shape[1:])
    return ortho, over.reshape(2, vectors, kept).swapaxes(1, 2)


def solution(mesh):
    placed = (
        P(None, None, None, None, "ta", None),
        P("ba", None, None, None, "ta", None),
        P(None, None, None, None, "ta", None),
        P(None, None, None, None, "ta", None),
    )

    return jax.shard_map(
        per_device,
        mesh=mesh,
        in_specs=placed,
        out_specs=(P("ba", None, None, None, "ta", None), P(None, "ba", None)),
        check_vma=False,
    )
```

```python
import functools

import jax
import jax.numpy as jnp
from jax import lax
from jax.experimental import pallas as pl
from jax.experimental.pallas import tpu as pltpu
from jax.sharding import PartitionSpec as P


HOPPING = 0.13
LANES = 128
HALVES = 2
COMPS = 12
PROJECT = (
    ((1, 1), (0, 1)),
    ((1, 0), (0, 2)),
    ((0, 1), (1, 3)),
    ((0, 2), (1, 2)),
)
REBUILD = (
    ((1, 3), (0, 3)),
    ((1, 0), (0, 2)),
    ((0, 3), (1, 1)),
    ((0, 2), (1, 2)),
)


def add_phase(left, right, phase):
    a, b = left
    c, d = right
    phase %= 4
    if phase == 0:
        return a + c, b + d
    if phase == 1:
        return a - d, b + c
    if phase == 2:
        return a - c, b - d
    return a + d, b - c


def plus(left, right):
    return left[0] + right[0], left[1] + right[1]


def minus(left, right):
    return left[0] - right[0], left[1] - right[1]


def rolled(value, shift, axis):
    shift %= value.shape[axis]
    return pltpu.roll(value, shift, axis) if shift else value


class Lattice:
    def __init__(self, slices, sites):
        self.slices = slices
        self.side = round(sites ** (1 / 3))
        self.rows = slices * sites // LANES
        self.shape = (self.rows, LANES)
        if self.side**3 != sites or LANES % (self.side * self.side) or COMPS % slices:
            raise ValueError("lattice shape")

    def masks(self):
        lane = lax.broadcasted_iota(jnp.int32, self.shape, 1)
        row = lax.broadcasted_iota(jnp.int32, self.shape, 0)
        side = self.side
        self.time = row % self.slices
        self.x_low = lane // (side * side)
        self.y = lane // side % side
        self.z = lane % side

    def shift(self, value, direction, ahead):
        side, area = self.side, self.side * self.side
        if direction == 0:
            step = 1 if ahead else -1
            edge = self.x_low == (0 if ahead else LANES // area - 1)
            mixed = jnp.where(edge, rolled(value, -step * self.slices, 0), value)
            return rolled(mixed, -step * area, 1)
        if direction < 3:
            place, unit = (self.y, side) if direction == 1 else (self.z, 1)
            edge = place == (side - 1 if ahead else 0)
            step = unit if ahead else -unit
            return jnp.where(
                edge, rolled(value, (side - 1) * step, 1), rolled(value, -step, 1)
            )
        if ahead:
            return jnp.where(self.time == self.slices - 1, 0.0, rolled(value, -1, 0))
        return jnp.where(self.time == 0, 0.0, rolled(value, 1, 0))


def load_spinor(ref, vector):
    def at(spin, colour):
        place = vector * (2 * COMPS) + spin * 3 + colour
        return ref[place], ref[place + COMPS]

    return at


def link_at(links, direction):
    def at(row, column):
        place = direction * 18 + row * 3 + column
        u, v = links[place], links[place + 9]
        return u, v + u, v - u

    return at


def entry_sums(values, size, sums):
    for matrix in range(values.shape[0] // (2 * size)):
        for entry in range(size):
            u = values[matrix * 2 * size + entry]
            v = values[matrix * 2 * size + size + entry]
            sums[matrix * 2 * size + entry] = v + u
            sums[matrix * 2 * size + size + entry] = v - u


def summed_link_at(links, sums, direction):
    def at(row, column):
        place = direction * 18 + row * 3 + column
        return links[place], sums[place], sums[place + 9]

    return at


def sums_of(halves):
    return [[(a, b, a + b) for a, b in half] for half in halves]


def times_link(link, halves):
    out = [[None] * 3 for _ in halves]
    for row in range(3):
        totals = [None] * len(halves)
        for column in range(3):
            u, s, d = link(row, column)
            for which, half in enumerate(halves):
                a, b, ab = half[column]
                terms = (u * ab, s * b, d * a)
                old = totals[which]
                totals[which] = terms if old is None else [x + y for x, y in zip(old, terms)]
        for which, (both, re, im) in enumerate(totals):
            out[which][row] = (both - re, both + im)
    return out


def times_dagger(link, halves):
    out = [[None] * 3 for _ in halves]
    for row in range(3):
        totals = [None] * len(halves)
        for column in range(3):
            u, s, d = link(column, row)
            for which, half in enumerate(halves):
                a, b, ab = half[column]
                terms = (u * ab, d * b, s * a)
                old = totals[which]
                totals[which] = terms if old is None else [x + y for x, y in zip(old, terms)]
        for which, (both, re, im) in enumerate(totals):
            out[which][row] = (both + re, both - im)
    return out


def half_spinor(spinor, direction, spin, ahead):
    other, phase = PROJECT[direction][spin]
    phase = phase if ahead else phase + 2
    return [add_phase(spinor(spin, c), spinor(2 + other, c), phase) for c in range(3)]


def pack_rim(lattice, spinor, links, direction, ahead_ref, behind_ref, vector):
    slices = lattice.slices
    ahead = half_spinor(spinor, 3, 0, True) + half_spinor(spinor, 3, 1, True)
    halves = [half_spinor(spinor, 3, spin, False) for spin in range(2)]
    behind = times_dagger(link_at(links, direction), sums_of(halves))
    behind = behind[0] + behind[1]
    for values, origin, ref in ((ahead, 0, ahead_ref), (behind, slices - 1, behind_ref)):
        flat = [part for pair in values for part in pair]
        for group in range(COMPS // slices):
            tile = None
            for place in range(slices):
                moved = rolled(flat[group * slices + place], place - origin, 0)
                tile = moved if tile is None else jnp.where(lattice.time == place, moved, tile)
            ref[vector * (COMPS // slices) + group] = tile


def unpack_rim(lattice, ref, vector, ahead, sign):
    slices = lattice.slices
    target = slices - 1 if ahead else 0
    flat = []
    for comp in range(COMPS):
        tile = ref[vector * (COMPS // slices) + comp // slices]
        moved = rolled(tile, target - comp % slices, 0)
        flat.append(jnp.where(lattice.time == target, moved * sign, 0.0))
    return [(flat[2 * i], flat[2 * i + 1]) for i in range(COMPS // 2)]


def open_kernel(
    lattice, groups, vectors, kept, ship,
    psi_ref, links_ref, basis, *refs,
):
    rims, refs = refs[: 2 * HALVES], refs[2 * HALVES :]
    pieces = refs[: groups - 1]
    psi, links, held, sems = refs[groups - 1 :]
    here = lax.axis_index("ba")
    rows, per = lattice.rows, basis.shape[2] // groups
    count = links.shape[0]
    fields = pltpu.make_async_copy(psi_ref, psi, sems.at[0])
    links_in = pltpu.make_async_copy(links_ref.at[pl.ds(3 * count, count)], links, sems.at[1])
    kept_in = []
    for step in range(1, groups if ship else 1):
        start = pl.multiple_of(partner(here, step, groups) * per, rows)
        kept_in.append(
            pltpu.make_async_copy(
                basis.at[:, :, pl.ds(start, held.shape[3]), :], held.at[step - 1], sems.at[1 + step]
            )
        )
    for copy in (links_in, fields, *kept_in):
        copy.start()
    lattice.masks()
    links_in.wait()
    fields.wait()

    size = vectors // HALVES
    for which in range(HALVES):

        def body(vector, carry, which=which):
            spinor = load_spinor(psi, which * size + vector)
            pack_rim(lattice, spinor, links, 0, rims[2 * which], rims[2 * which + 1], vector)
            return carry

        lax.fori_loop(0, size, body, 0)
    for step, copy in enumerate(kept_in):
        copy.wait()

        def turn(group, carry, step=step):
            first = pl.multiple_of(group * 8, 8)
            for ri in range(2):
                for start in range(0, ship, rows):
                    tile = held[step, pl.ds(first, 8), ri, start : start + rows, :]
                    tile = jnp.swapaxes(tile, 0, 1)
                    size = min(rows, ship - start)
                    pieces[step][start : start + size, pl.ds(ri * kept + first, 8), :] = tile[:size]
            return carry

        lax.fori_loop(0, kept // 8, turn, 0)


def basis_kernel(rows, kept, basis, out):
    def body(tile, carry):
        blocks = pl.ds(pl.multiple_of(tile * rows, rows), rows)
        for ri in range(2):
            for first in range(0, kept, 16):
                value = jnp.swapaxes(basis[first : first + 16, ri, blocks, :], 0, 1)
                high, low = two_halves(value)
                start = ri * kept + first
                out[blocks, start : start + 16, :] = high
                out[blocks, 2 * kept + start : 2 * kept + start + 16, :] = low
        return carry

    lax.fori_loop(0, basis.shape[2] // rows, body, 0)


def local_kernel(lattice, vectors, base, psi, links, clover, out, link_sums, clover_sums):
    lattice.masks()
    entry_sums(links, 9, link_sums)
    entry_sums(clover, 36, clover_sums)

    def body(vector, carry):
        spinor = load_spinor(psi, base + vector)
        upper = [[None] * 3 for _ in range(2)]
        lower = [[None] * 3 for _ in range(2)]
        for direction in range(4):
            link = summed_link_at(links, link_sums, direction)
            halves = []
            for spin in range(2):
                half = half_spinor(spinor, direction, spin, True)
                halves.append([tuple(lattice.shift(p, direction, True) for p in h) for h in half])
            aheads = times_link(link, sums_of(halves))
            halves = [half_spinor(spinor, direction, spin, False) for spin in range(2)]
            behinds = times_dagger(link, sums_of(halves))
            for spin in range(2):
                ahead = aheads[spin]
                behind = [
                    tuple(lattice.shift(p, direction, False) for p in h) for h in behinds[spin]
                ]
                place, phase = REBUILD[direction][spin]
                for c in range(3):
                    total, diff = plus(ahead[c], behind[c]), minus(ahead[c], behind[c])
                    if upper[spin][c] is None:
                        upper[spin][c] = total
                    else:
                        upper[spin][c] = plus(upper[spin][c], total)
                    if lower[place][c] is None:
                        zero = jnp.zeros_like(diff[0])
                        lower[place][c] = add_phase((zero, zero), diff, phase)
                    else:
                        lower[place][c] = add_phase(lower[place][c], diff, phase)
        for chiral, hops in ((0, upper), (1, lower)):
            field = [spinor(2 * chiral + i // 3, i % 3) for i in range(6)]
            field = [(x, y, x + y) for x, y in field]
            for row in range(6):
                total = None
                for column in range(6):
                    place = chiral * 72 + row * 6 + column
                    a, b, ab = field[column]
                    terms = (
                        clover[place] * ab,
                        clover_sums[place] * b,
                        clover_sums[place + 36] * a,
                    )
                    total = terms if total is None else [x + y for x, y in zip(total, terms)]
                both, re, im = total
                place = vector * (2 * COMPS) + chiral * 6 + row
                out[place] = both - re - HOPPING * hops[row // 3][row % 3][0]
                out[place + COMPS] = both + im - HOPPING * hops[row // 3][row % 3][1]
        return carry

    lax.fori_loop(0, vectors, body, 0)


def rim_signs():
    count, here = lax.axis_size("ta"), lax.axis_index("ta")
    one = jnp.float32(1.0)
    return jnp.where(here == count - 1, -one, one), jnp.where(here == 0, -one, one)


def finish(lattice, links, part, rim_ahead, rim_behind, vector, signs, store):
    ahead_all = unpack_rim(lattice, rim_ahead, vector, True, signs[0])
    behind_all = unpack_rim(lattice, rim_behind, vector, False, signs[1])
    both = times_link(link_at(links, 3), sums_of([ahead_all[:3], ahead_all[3:]]))
    for spin in range(2):
        ahead = both[spin]
        behind = behind_all[3 * spin : 3 * spin + 3]
        for c in range(3):
            for ri in range(2):
                f, b = ahead[c][ri], behind[c][ri]
                place = vector * (2 * COMPS) + ri * COMPS + spin * 3 + c
                store(place, part[place] - HOPPING * (f + b))
                store(place + 6, -(part[place + 6] + HOPPING * (f - b)))


def middle_kernel(
    lattice, vectors, part, links, rim_ahead, rim_behind, out, ahead_ref, behind_ref
):
    lattice.masks()
    signs = rim_signs()

    def body(vector, carry):
        def store(place, value):
            out[place] = value

        finish(lattice, links, part, rim_ahead, rim_behind, vector, signs, store)
        pack_rim(lattice, load_spinor(out, vector), links, 3, ahead_ref, behind_ref, vector)
        return carry

    lax.fori_loop(0, vectors, body, 0)


def two_halves(value):
    high = value.astype(jnp.bfloat16)
    return high, (value - high.astype(jnp.float32)).astype(jnp.bfloat16)


def pair_of(ref, block):
    return jnp.concatenate([ref[block], ref[block + 1]], axis=1)


def row_pairs(ref, block):
    return jnp.concatenate(two_halves(pair_of(ref, block)), axis=0)


def correlate_kernel(
    lattice, size, kept, scale, part, links, rim_ahead, rim_behind, basis, *refs,
):
    earlier, (applied, over, field) = refs[:-3], refs[-3:]
    lattice.masks()
    signs = rim_signs()
    rows = lattice.rows

    def body(vector, carry):
        def store(place, value):
            field[place] = value

        finish(lattice, links, part, rim_ahead, rim_behind, vector, signs, store)
        return carry

    lax.fori_loop(0, size, body, 0)

    def add(comp, total):
        blocks_here = pl.ds(pl.multiple_of(comp * rows, rows), rows)
        for ri in range(2):
            for first in range(0, size, 8):
                count = min(8, size - first)
                tiles = jnp.stack(
                    [field[(first + i) * 2 * COMPS + ri * COMPS + comp] for i in range(count)]
                )
                start = ri * size + first
                applied[blocks_here, start : start + count, :] = jnp.swapaxes(tiles, 0, 1)
        for place in range(0, rows, 2):
            block = comp * rows + place
            total = total + lax.dot_general(
                row_pairs(applied, block),
                pair_of(basis, block),
                (((1,), (1,)), ((), ())),
                preferred_element_type=jnp.float32,
            )
        return total

    total = lax.fori_loop(0, COMPS, add, jnp.zeros((4 * size, 4 * kept), jnp.float32))
    total = total[: 2 * size] + total[2 * size :]
    total = total[:, : 2 * kept] + total[:, 2 * kept :]
    real, imag = total[:size], total[size:]
    real, imag = (
        scale * (real[:, :kept] + imag[:, kept:]),
        scale * (imag[:, :kept] - real[:, kept:]),
    )
    shares = len(earlier) + 1
    for which, ref in enumerate(earlier):
        over[which * size : (which + 1) * size, :] = ref[:size, :]
        over[(shares + which) * size : (shares + which + 1) * size, :] = ref[size:, :]
    over[(shares - 1) * size : shares * size, :] = real
    over[(2 * shares - 1) * size :, :] = imag


def partner(here, step, count):
    if count & (count - 1) == 0:
        return here ^ step
    return (here + step) % count


def source(here, step, count):
    if count & (count - 1) == 0:
        return here ^ step
    return (here + count - step) % count


def exchanged(values, axis):
    count = lax.axis_size(axis)
    out = [values[0]]
    for step in range(1, count):
        pairs = [(i, partner(i, step, count)) for i in range(count)]
        out.append(lax.ppermute(values[step], axis, pairs))
    return out


def summed(value, axis, radix):
    count = lax.axis_size(axis)
    if count & (count - 1):
        return lax.psum(value, axis)
    stride = 1
    while stride < count:
        size, radix = min(radix[0], count // stride), radix[1:] or radix
        total = value
        for step in range(1, size):
            total = total + lax.ppermute(
                value, axis, [(i, i ^ (step * stride)) for i in range(count)]
            )
        value = total
        stride *= size
    return value


def weight_rows(real, imag):
    weight = jnp.concatenate(
        [jnp.concatenate([real, -imag], axis=1), jnp.concatenate([imag, real], axis=1)], axis=0
    )
    high, low = two_halves(weight)
    return jnp.concatenate(
        [jnp.concatenate([high, high], axis=1), jnp.concatenate([low, low], axis=1)], axis=0
    )


def weighted(weight, basis):
    both = jnp.dot(weight, basis, preferred_element_type=jnp.float32)
    half = both.shape[0] // 2
    return both[:half] + both[half:]


def project_kernel(groups, vectors, kept, ship, over, basis, *outs):
    here = lax.axis_index("ba")
    per = basis.shape[0] // groups
    weight = weight_rows(over[:vectors, :], over[vectors:, :])
    for step in range(groups):
        first = partner(here, step, groups) * per + ship
        for block in range(0, per - ship, 2):
            value = weighted(weight, pair_of(basis, first + block))
            outs[step][block] = value[:, :LANES]
            outs[step][block + 1] = value[:, LANES:]
        outs[step][per - ship] = jnp.zeros((2 * vectors, LANES), jnp.float32)
        outs[step][per - ship, :, :kept] = over[...]


def rest_kernel(groups, vectors, kept, ship, scale, over, basis, *refs):
    shares, refs = refs[:HALVES], refs[HALVES:]
    parts, refs = refs[:groups], refs[groups:]
    size = vectors // HALVES
    pieces, (rest_ref, gram) = refs[:-2], refs[-2:]
    here = lax.axis_index("ba")
    per = basis.shape[0] // groups
    weights = [weight_rows(over[:vectors, :], over[vectors:, :])]
    for part in parts[1:]:
        there = part[per - ship, :, :kept]
        weights.append(weight_rows(there[:vectors], there[vectors:]))
    full = None
    for block in range(0, per, 2):
        mine = here * per + block
        if block < ship:
            total = weighted(weights[0], pair_of(basis, mine))
            for weight, piece in zip(weights[1:], pieces):
                total = total + weighted(weight, row_pairs(piece, block))
        else:
            total = [
                sum((part[block + i - ship] for part in parts[1:]), parts[0][block + i - ship])
                for i in range(2)
            ]
            total = jnp.concatenate(total, axis=1)
        rows = [pair_of(share, mine) for share in shares]
        rows = [r[:size] for r in rows] + [r[size:] for r in rows]
        rest = jnp.concatenate(rows, axis=0) - total
        rest_ref[block] = rest[:, :LANES]
        rest_ref[block + 1] = rest[:, LANES:]
        both = jnp.concatenate(two_halves(rest), axis=0)
        term = lax.dot_general(
            both, both, (((1,), (1,)), ((), ())), preferred_element_type=jnp.float32
        )
        full = term if full is None else full + term
    full = full[: 2 * vectors] + full[2 * vectors :]
    full = full[:, : 2 * vectors] + full[:, 2 * vectors :]
    real, imag = full[:vectors], full[vectors:]
    gram[:, :vectors] = scale * (real[:, :vectors] + imag[:, vectors:])
    gram[:, vectors:] = scale * (real[:, vectors:] - imag[:, :vectors])


def ortho_kernel(groups, vectors, gram, rest, *refs):
    here = lax.axis_index("ba")
    outs, work = refs[:-1], refs[-1]
    shape = (vectors, 2 * vectors)
    row = lax.broadcasted_iota(jnp.int32, shape, 0)
    lane = lax.broadcasted_iota(jnp.int32, shape, 1)
    unit = jnp.where(lane == row + vectors, 1.0, 0.0)
    re = jnp.where(lane < vectors, gram[...], unit)
    im = jnp.concatenate([gram[:, vectors:], jnp.zeros((vectors, vectors), jnp.float32)], axis=1)
    pivots = jnp.ones(shape, jnp.float32)
    for pivot in range(vectors):
        row_re, row_im = re[pivot : pivot + 1], im[pivot : pivot + 1]
        col_re = jnp.broadcast_to(re[:, pivot : pivot + 1], shape)
        col_im = jnp.broadcast_to(im[:, pivot : pivot + 1], shape)
        value = col_re[pivot : pivot + 1]
        inverse = 1.0 / value
        below = row > pivot
        col_re = jnp.where(below, col_re * inverse, 0.0)
        col_im = jnp.where(below, col_im * inverse, 0.0)
        pivots = jnp.where(row == pivot, value, pivots)
        re, im = (
            re - (col_re * row_re - col_im * row_im),
            im - (col_re * row_im + col_im * row_re),
        )
    roots = 1.0 / jnp.sqrt(pivots)
    inv_re, inv_im = (re * roots)[:, vectors:], (im * roots)[:, vectors:]
    own = vectors // groups
    for group in range(groups):
        rows = slice(group * own, (group + 1) * own)
        work[group, :own, :vectors] = inv_re[rows]
        work[group, :own, vectors:] = inv_im[rows]
        work[group, own:, :vectors] = -inv_im[rows]
        work[group, own:, vectors:] = inv_re[rows]
    weight = jnp.concatenate(
        [work[partner(here, step, groups)] for step in range(groups)], axis=0
    )
    high, low = two_halves(weight)
    weight = jnp.concatenate(
        [jnp.concatenate([high, high], axis=1), jnp.concatenate([low, low], axis=1)], axis=0
    )
    for block in range(0, rest.shape[0], 2):
        full = weighted(weight, row_pairs(rest, block))
        for step in range(groups):
            rows = slice(step * 2 * own, (step + 1) * 2 * own)
            outs[step][block] = full[rows, :LANES]
            outs[step][block + 1] = full[rows, LANES:]


def place_kernel(groups, own, rows, *refs):
    parts, out = refs[:groups], refs[groups]
    here = lax.axis_index("ba")
    per = parts[0].shape[0]
    for step in range(groups):
        first = source(here, step, groups) * per
        if per % rows:
            for block in range(per):
                for ri in range(2):
                    out[:, ri, first + block, :] = parts[step][block, ri * own : (ri + 1) * own, :]
        else:
            for block in range(0, per, rows):
                tile = jnp.swapaxes(parts[step][block : block + rows], 0, 1)
                there = pl.ds(pl.multiple_of(first + block, rows), rows)
                for ri in range(2):
                    out[:, ri, there, :] = tile[ri * own : (ri + 1) * own]


def call(kernel, outs, *args, scratch=(), flops=0, grant=6, remote=()):
    nbytes = sum(a.size * a.dtype.itemsize for a in (*args, *outs))
    spec = pl.BlockSpec(memory_space=pltpu.VMEM)
    anywhere = pl.BlockSpec(memory_space=pltpu.HBM)
    return pl.pallas_call(
        kernel,
        out_shape=tuple(outs),
        in_specs=[anywhere if i in remote else spec for i in range(len(args))],
        out_specs=tuple([spec] * len(outs)),
        scratch_shapes=list(scratch),
        compiler_params=pltpu.CompilerParams(vmem_limit_bytes=grant << 20),
        cost_estimate=pl.CostEstimate(flops=flops, bytes_accessed=nbytes, transcendentals=0),
    )(*args)


def shape_of(*dims):
    return jax.ShapeDtypeStruct(dims, jnp.float32)


def tiles_of(value, leading):
    slices, sites = value.shape[-2:]
    value = value.reshape(leading, slices, sites // LANES, LANES)
    return value.swapaxes(1, 2).reshape(leading, slices * sites // LANES, LANES)


def per_device(search_block, kept_basis, gauge_links, clover_term):
    vectors, kept = search_block.shape[0], kept_basis.shape[0]
    slices, sites = search_block.shape[-2:]
    groups, places = lax.axis_size("ba"), lax.axis_size("ta")
    lattice = Lattice(slices, sites)
    rows = lattice.rows
    blocks = COMPS * rows
    per = blocks // groups
    own = vectors // groups
    scale = 1.0 / (2 * COMPS * slices * sites * places)
    psi = tiles_of(search_block, vectors * 2 * COMPS)
    basis = tiles_of(kept_basis, kept * 2 * COMPS).reshape(kept, 2, blocks, LANES)
    ship = per * 5 // 24 * 2 if per % rows == 0 else 0
    links = tiles_of(gauge_links, 72)
    clover = tiles_of(clover_term, 144)
    size = vectors // HALVES
    rim = shape_of(size * COMPS // slices, rows, LANES)
    field = shape_of(size * 2 * COMPS, rows, LANES)
    work = size * rows * LANES
    in_hbm = functools.partial(pltpu.with_memory_space_constraint, memory_space=pltpu.HBM)

    def swap(ahead, behind):
        down = [(i, (i + places - 1) % places) for i in range(places)]
        up = [(i, (i + 1) % places) for i in range(places)]
        return lax.ppermute(ahead, "ta", down), lax.ppermute(behind, "ta", up)

    def local(values, base):
        return call(
            functools.partial(local_kernel, lattice, size, base),
            (field,),
            values,
            links,
            clover,
            scratch=[pltpu.VMEM(links.shape, jnp.float32), pltpu.VMEM(clover.shape, jnp.float32)],
            flops=2000 * work,
        )[0]

    opened = call(
        functools.partial(open_kernel, lattice, groups, vectors, kept, ship),
        (rim,) * (2 * HALVES) + (shape_of(max(ship, 1), 2 * kept, LANES),) * (groups - 1),
        in_hbm(psi),
        in_hbm(links),
        in_hbm(basis),
        scratch=[
            pltpu.VMEM(psi.shape, jnp.float32),
            pltpu.VMEM((18, rows, LANES), jnp.float32),
            pltpu.VMEM((groups - 1, kept, 2, -(-ship // rows) * rows or rows, LANES), jnp.float32),
            pltpu.SemaphoreType.DMA((groups + 1,)),
        ],
        flops=400 * work,
        grant=8,
        remote=(0, 1, 2),
    )
    rims = [swap(opened[2 * which], opened[2 * which + 1]) for which in range(HALVES)]
    pieces = exchanged([None, *opened[2 * HALVES :]], "ba")[1:] if ship else []
    parts = []
    for which in range(HALVES):
        part = local(psi, which * size)
        first, ahead, behind = call(
            functools.partial(middle_kernel, lattice, size),
            (field, rim, rim),
            part,
            links,
            *rims[which],
            flops=400 * work,
        )
        rims[which] = swap(ahead, behind)
        parts.append(first)
    (basis_rows,) = call(
        functools.partial(basis_kernel, rows, kept),
        (jax.ShapeDtypeStruct((blocks, 4 * kept, LANES), jnp.bfloat16),),
        basis,
    )
    parts = [local(first, 0) for first in parts]
    applied, overs = [], []
    for which in range(HALVES):
        earlier = overs if which == HALVES - 1 else []
        share, over = call(
            functools.partial(correlate_kernel, lattice, size, kept, scale),
            (shape_of(blocks, 2 * size, LANES), shape_of(2 * size * (len(earlier) + 1), kept)),
            parts[which],
            links,
            *rims[which],
            basis_rows,
            *earlier,
            scratch=[pltpu.VMEM((size * 2 * COMPS, rows, LANES), jnp.float32)],
            flops=400 * work,
        )
        applied.append(share)
        overs.append(over)
    over = summed(over, "ta", (2, 4))
    parts = call(
        functools.partial(project_kernel, groups, vectors, kept, ship),
        (shape_of(per - ship + 1, 2 * vectors, LANES),) * groups,
        over,
        basis_rows,
    )
    parts = exchanged(parts, "ba")
    rest, gram = call(
        functools.partial(rest_kernel, groups, vectors, kept, ship, scale),
        (shape_of(per, 2 * vectors, LANES), shape_of(vectors, 2 * vectors)),
        over,
        basis_rows,
        *applied,
        *parts,
        *pieces,
    )
    gram = summed(summed(gram, "ta", (2, 4)), "ba", (4,))
    piece = shape_of(per, 2 * own, LANES)
    pieces = call(
        functools.partial(ortho_kernel, groups, vectors),
        (piece,) * groups,
        gram,
        rest,
        scratch=[pltpu.VMEM((groups, 2 * own, 2 * vectors), jnp.float32)],
    )
    pieces = exchanged(pieces, "ba")
    (ortho,) = call(
        functools.partial(place_kernel, groups, own, rows),
        (shape_of(own, 2, blocks, LANES),),
        *pieces,
    )
    ortho = ortho.reshape(own * 2 * COMPS, sites // LANES, slices, LANES).swapaxes(1, 2)
    ortho = ortho.reshape(own, *search_block.shape[1:])
    return ortho, over.reshape(2, vectors, kept).swapaxes(1, 2)


def solution(mesh):
    placed = (
        P(None, None, None, None, "ta", None),
        P("ba", None, None, None, "ta", None),
        P(None, None, None, None, "ta", None),
        P(None, None, None, None, "ta", None),
    )


    return jax.shard_map(
        per_device,
        mesh=mesh,
        in_specs=placed,
        out_specs=(P("ba", None, None, None, "ta", None), P(None, "ba", None)),
        check_vma=False,
    )
```

```python
import functools

import jax
import jax.numpy as jnp
from jax import lax
from jax.experimental import pallas as pl
from jax.experimental.pallas import tpu as pltpu
from jax.sharding import PartitionSpec as P


HOPPING = 0.13
LANES = 128
HALVES = 1
COMPS = 12
PROJECT = (
    ((1, 1), (0, 1)),
    ((1, 0), (0, 2)),
    ((0, 1), (1, 3)),
    ((0, 2), (1, 2)),
)
REBUILD = (
    ((1, 3), (0, 3)),
    ((1, 0), (0, 2)),
    ((0, 3), (1, 1)),
    ((0, 2), (1, 2)),
)


def add_phase(left, right, phase):
    a, b = left
    c, d = right
    phase %= 4
    if phase == 0:
        return a + c, b + d
    if phase == 1:
        return a - d, b + c
    if phase == 2:
        return a - c, b - d
    return a + d, b - c


def plus(left, right):
    return left[0] + right[0], left[1] + right[1]


def minus(left, right):
    return left[0] - right[0], left[1] - right[1]


def rolled(value, shift, axis):
    shift %= value.shape[axis]
    return pltpu.roll(value, shift, axis) if shift else value


class Lattice:
    def __init__(self, slices, sites):
        self.slices = slices
        self.side = round(sites ** (1 / 3))
        self.rows = slices * sites // LANES
        self.shape = (self.rows, LANES)
        if self.side**3 != sites or LANES % (self.side * self.side) or COMPS % slices:
            raise ValueError("lattice shape")

    def masks(self):
        lane = lax.broadcasted_iota(jnp.int32, self.shape, 1)
        row = lax.broadcasted_iota(jnp.int32, self.shape, 0)
        side = self.side
        self.time = row % self.slices
        self.x_low = lane // (side * side)
        self.y = lane // side % side
        self.z = lane % side

    def shift(self, value, direction, ahead):
        side, area = self.side, self.side * self.side
        if direction == 0:
            step = 1 if ahead else -1
            edge = self.x_low == (0 if ahead else LANES // area - 1)
            mixed = jnp.where(edge, rolled(value, -step * self.slices, 0), value)
            return rolled(mixed, -step * area, 1)
        if direction < 3:
            place, unit = (self.y, side) if direction == 1 else (self.z, 1)
            edge = place == (side - 1 if ahead else 0)
            step = unit if ahead else -unit
            return jnp.where(
                edge, rolled(value, (side - 1) * step, 1), rolled(value, -step, 1)
            )
        if ahead:
            return jnp.where(self.time == self.slices - 1, 0.0, rolled(value, -1, 0))
        return jnp.where(self.time == 0, 0.0, rolled(value, 1, 0))


def load_spinor(ref, vector):
    def at(spin, colour):
        place = vector * (2 * COMPS) + spin * 3 + colour
        return ref[place], ref[place + COMPS]

    return at


def link_at(links, direction):
    def at(row, column):
        place = direction * 18 + row * 3 + column
        u, v = links[place], links[place + 9]
        return u, v + u, v - u

    return at


def entry_sums(values, size, sums):
    for matrix in range(values.shape[0] // (2 * size)):
        for entry in range(size):
            u = values[matrix * 2 * size + entry]
            v = values[matrix * 2 * size + size + entry]
            sums[matrix * 2 * size + entry] = v + u
            sums[matrix * 2 * size + size + entry] = v - u


def summed_link_at(links, sums, direction):
    def at(row, column):
        place = direction * 18 + row * 3 + column
        return links[place], sums[place], sums[place + 9]

    return at


def sums_of(halves):
    return [[(a, b, a + b) for a, b in half] for half in halves]


def times_link(link, halves):
    out = [[None] * 3 for _ in halves]
    for row in range(3):
        totals = [None] * len(halves)
        for column in range(3):
            u, s, d = link(row, column)
            for which, half in enumerate(halves):
                a, b, ab = half[column]
                terms = (u * ab, s * b, d * a)
                old = totals[which]
                totals[which] = terms if old is None else [x + y for x, y in zip(old, terms)]
        for which, (both, re, im) in enumerate(totals):
            out[which][row] = (both - re, both + im)
    return out


def times_dagger(link, halves):
    out = [[None] * 3 for _ in halves]
    for row in range(3):
        totals = [None] * len(halves)
        for column in range(3):
            u, s, d = link(column, row)
            for which, half in enumerate(halves):
                a, b, ab = half[column]
                terms = (u * ab, d * b, s * a)
                old = totals[which]
                totals[which] = terms if old is None else [x + y for x, y in zip(old, terms)]
        for which, (both, re, im) in enumerate(totals):
            out[which][row] = (both + re, both - im)
    return out


def half_spinor(spinor, direction, spin, ahead):
    other, phase = PROJECT[direction][spin]
    phase = phase if ahead else phase + 2
    return [add_phase(spinor(spin, c), spinor(2 + other, c), phase) for c in range(3)]


def pack_rim(lattice, spinor, links, direction, ahead_ref, behind_ref, vector):
    slices = lattice.slices
    ahead = half_spinor(spinor, 3, 0, True) + half_spinor(spinor, 3, 1, True)
    halves = [half_spinor(spinor, 3, spin, False) for spin in range(2)]
    behind = times_dagger(link_at(links, direction), sums_of(halves))
    behind = behind[0] + behind[1]
    for values, origin, ref in ((ahead, 0, ahead_ref), (behind, slices - 1, behind_ref)):
        flat = [part for pair in values for part in pair]
        for group in range(COMPS // slices):
            tile = None
            for place in range(slices):
                moved = rolled(flat[group * slices + place], place - origin, 0)
                tile = moved if tile is None else jnp.where(lattice.time == place, moved, tile)
            ref[vector * (COMPS // slices) + group] = tile


def unpack_rim(lattice, ref, vector, ahead, sign):
    slices = lattice.slices
    target = slices - 1 if ahead else 0
    flat = []
    for comp in range(COMPS):
        tile = ref[vector * (COMPS // slices) + comp // slices]
        moved = rolled(tile, target - comp % slices, 0)
        flat.append(jnp.where(lattice.time == target, moved * sign, 0.0))
    return [(flat[2 * i], flat[2 * i + 1]) for i in range(COMPS // 2)]


def open_kernel(
    lattice, groups, vectors, kept, ship,
    psi_ref, links_ref, basis, *refs,
):
    rims, refs = refs[: 2 * HALVES], refs[2 * HALVES :]
    pieces = refs[: groups - 1]
    psi, links, held, sems = refs[groups - 1 :]
    here = lax.axis_index("ba")
    rows, per = lattice.rows, basis.shape[2] // groups
    count = links.shape[0]
    fields = pltpu.make_async_copy(psi_ref, psi, sems.at[0])
    links_in = pltpu.make_async_copy(links_ref.at[pl.ds(3 * count, count)], links, sems.at[1])
    kept_in = []
    for step in range(1, groups if ship else 1):
        start = pl.multiple_of(partner(here, step, groups) * per, rows)
        kept_in.append(
            pltpu.make_async_copy(
                basis.at[:, :, pl.ds(start, held.shape[3]), :], held.at[step - 1], sems.at[1 + step]
            )
        )
    for copy in (links_in, fields, *kept_in):
        copy.start()
    lattice.masks()
    links_in.wait()
    fields.wait()

    size = vectors // HALVES
    for which in range(HALVES):

        def body(vector, carry, which=which):
            spinor = load_spinor(psi, which * size + vector)
            pack_rim(lattice, spinor, links, 0, rims[2 * which], rims[2 * which + 1], vector)
            return carry

        lax.fori_loop(0, size, body, 0)
    for step, copy in enumerate(kept_in):
        copy.wait()

        def turn(group, carry, step=step):
            first = pl.multiple_of(group * 8, 8)
            for ri in range(2):
                for start in range(0, ship, rows):
                    tile = held[step, pl.ds(first, 8), ri, start : start + rows, :]
                    tile = jnp.swapaxes(tile, 0, 1)
                    size = min(rows, ship - start)
                    pieces[step][start : start + size, pl.ds(ri * kept + first, 8), :] = tile[:size]
            return carry

        lax.fori_loop(0, kept // 8, turn, 0)


def basis_kernel(rows, kept, basis, out):
    def body(tile, carry):
        blocks = pl.ds(pl.multiple_of(tile * rows, rows), rows)
        for ri in range(2):
            for first in range(0, kept, 16):
                value = jnp.swapaxes(basis[first : first + 16, ri, blocks, :], 0, 1)
                high, low = two_halves(value)
                start = ri * kept + first
                out[blocks, start : start + 16, :] = high
                out[blocks, 2 * kept + start : 2 * kept + start + 16, :] = low
        return carry

    lax.fori_loop(0, basis.shape[2] // rows, body, 0)


def local_kernel(lattice, vectors, base, psi, links, clover, out, link_sums, clover_sums):
    lattice.masks()
    entry_sums(links, 9, link_sums)
    entry_sums(clover, 36, clover_sums)

    def body(vector, carry):
        spinor = load_spinor(psi, base + vector)
        upper = [[None] * 3 for _ in range(2)]
        lower = [[None] * 3 for _ in range(2)]
        for direction in range(4):
            link = summed_link_at(links, link_sums, direction)
            halves = []
            for spin in range(2):
                half = half_spinor(spinor, direction, spin, True)
                halves.append([tuple(lattice.shift(p, direction, True) for p in h) for h in half])
            aheads = times_link(link, sums_of(halves))
            halves = [half_spinor(spinor, direction, spin, False) for spin in range(2)]
            behinds = times_dagger(link, sums_of(halves))
            for spin in range(2):
                ahead = aheads[spin]
                behind = [
                    tuple(lattice.shift(p, direction, False) for p in h) for h in behinds[spin]
                ]
                place, phase = REBUILD[direction][spin]
                for c in range(3):
                    total, diff = plus(ahead[c], behind[c]), minus(ahead[c], behind[c])
                    if upper[spin][c] is None:
                        upper[spin][c] = total
                    else:
                        upper[spin][c] = plus(upper[spin][c], total)
                    if lower[place][c] is None:
                        zero = jnp.zeros_like(diff[0])
                        lower[place][c] = add_phase((zero, zero), diff, phase)
                    else:
                        lower[place][c] = add_phase(lower[place][c], diff, phase)
        for chiral, hops in ((0, upper), (1, lower)):
            field = [spinor(2 * chiral + i // 3, i % 3) for i in range(6)]
            field = [(x, y, x + y) for x, y in field]
            for row in range(6):
                total = None
                for column in range(6):
                    place = chiral * 72 + row * 6 + column
                    a, b, ab = field[column]
                    terms = (
                        clover[place] * ab,
                        clover_sums[place] * b,
                        clover_sums[place + 36] * a,
                    )
                    total = terms if total is None else [x + y for x, y in zip(total, terms)]
                both, re, im = total
                place = vector * (2 * COMPS) + chiral * 6 + row
                out[place] = both - re - HOPPING * hops[row // 3][row % 3][0]
                out[place + COMPS] = both + im - HOPPING * hops[row // 3][row % 3][1]
        return carry

    lax.fori_loop(0, vectors, body, 0)


def rim_signs():
    count, here = lax.axis_size("ta"), lax.axis_index("ta")
    one = jnp.float32(1.0)
    return jnp.where(here == count - 1, -one, one), jnp.where(here == 0, -one, one)


def finish(lattice, links, part, rim_ahead, rim_behind, vector, signs, store):
    ahead_all = unpack_rim(lattice, rim_ahead, vector, True, signs[0])
    behind_all = unpack_rim(lattice, rim_behind, vector, False, signs[1])
    both = times_link(link_at(links, 3), sums_of([ahead_all[:3], ahead_all[3:]]))
    for spin in range(2):
        ahead = both[spin]
        behind = behind_all[3 * spin : 3 * spin + 3]
        for c in range(3):
            for ri in range(2):
                f, b = ahead[c][ri], behind[c][ri]
                place = vector * (2 * COMPS) + ri * COMPS + spin * 3 + c
                store(place, part[place] - HOPPING * (f + b))
                store(place + 6, -(part[place + 6] + HOPPING * (f - b)))


def middle_kernel(
    lattice, vectors, part, links, rim_ahead, rim_behind, out, ahead_ref, behind_ref
):
    lattice.masks()
    signs = rim_signs()

    def body(vector, carry):
        def store(place, value):
            out[place] = value

        finish(lattice, links, part, rim_ahead, rim_behind, vector, signs, store)
        pack_rim(lattice, load_spinor(out, vector), links, 3, ahead_ref, behind_ref, vector)
        return carry

    lax.fori_loop(0, vectors, body, 0)


def two_halves(value):
    high = value.astype(jnp.bfloat16)
    return high, (value - high.astype(jnp.float32)).astype(jnp.bfloat16)


def pair_of(ref, block):
    return jnp.concatenate([ref[block], ref[block + 1]], axis=1)


def row_pairs(ref, block):
    return jnp.concatenate(two_halves(pair_of(ref, block)), axis=0)


def correlate_kernel(
    lattice, size, kept, scale, part, links, rim_ahead, rim_behind, basis, applied, over, field,
):
    lattice.masks()
    signs = rim_signs()
    rows = lattice.rows

    def body(vector, carry):
        def store(place, value):
            field[place] = value

        finish(lattice, links, part, rim_ahead, rim_behind, vector, signs, store)
        return carry

    lax.fori_loop(0, size, body, 0)

    def add(comp, total):
        blocks_here = pl.ds(pl.multiple_of(comp * rows, rows), rows)
        for ri in range(2):
            for first in range(0, size, 8):
                count = min(8, size - first)
                tiles = jnp.stack(
                    [field[(first + i) * 2 * COMPS + ri * COMPS + comp] for i in range(count)]
                )
                start = ri * size + first
                applied[blocks_here, start : start + count, :] = jnp.swapaxes(tiles, 0, 1)
        mine = jnp.concatenate([applied[comp * rows + i] for i in range(rows)], axis=1)
        kept_rows = jnp.concatenate([basis[comp * rows + i] for i in range(rows)], axis=1)
        return total + lax.dot_general(
            jnp.concatenate(two_halves(mine), axis=0),
            kept_rows,
            (((1,), (1,)), ((), ())),
            preferred_element_type=jnp.float32,
        )

    total = lax.fori_loop(0, COMPS, add, jnp.zeros((4 * size, 4 * kept), jnp.float32))
    total = total[: 2 * size] + total[2 * size :]
    total = total[:, : 2 * kept] + total[:, 2 * kept :]
    real, imag = total[:size], total[size:]
    real, imag = (
        scale * (real[:, :kept] + imag[:, kept:]),
        scale * (imag[:, :kept] - real[:, kept:]),
    )
    over[...] = packed(jnp.concatenate([real, imag], axis=0))


def partner(here, step, count):
    if count & (count - 1) == 0:
        return here ^ step
    return (here + step) % count


def source(here, step, count):
    if count & (count - 1) == 0:
        return here ^ step
    return (here + count - step) % count


def exchanged(values, axis):
    count = lax.axis_size(axis)
    out = [values[0]]
    for step in range(1, count):
        pairs = [(i, partner(i, step, count)) for i in range(count)]
        out.append(lax.ppermute(values[step], axis, pairs))
    return out


def summed(value, axis, radix):
    count = lax.axis_size(axis)
    if count & (count - 1):
        return lax.psum(value, axis)
    stride = 1
    while stride < count:
        size, radix = min(radix[0], count // stride), radix[1:] or radix
        total = value
        for step in range(1, size):
            total = total + lax.ppermute(
                value, axis, [(i, i ^ (step * stride)) for i in range(count)]
            )
        value = total
        stride *= size
    return value


def packed(value):
    count = LANES // value.shape[1]
    size = value.shape[0] // count
    return jnp.concatenate([value[i * size : (i + 1) * size] for i in range(count)], axis=1)


def unpacked(value, width):
    return jnp.concatenate(
        [value[:, i * width : (i + 1) * width] for i in range(LANES // width)], axis=0
    )


def weight_rows(real, imag):
    weight = jnp.concatenate(
        [jnp.concatenate([real, -imag], axis=1), jnp.concatenate([imag, real], axis=1)], axis=0
    )
    high, low = two_halves(weight)
    return jnp.concatenate(
        [jnp.concatenate([high, high], axis=1), jnp.concatenate([low, low], axis=1)], axis=0
    )


def weighted(weight, basis):
    both = jnp.dot(weight, basis, preferred_element_type=jnp.float32)
    half = both.shape[0] // 2
    return both[:half] + both[half:]


def project_kernel(groups, vectors, kept, ship, over, basis, *outs):
    here = lax.axis_index("ba")
    per = basis.shape[0] // groups
    mine = unpacked(over[...], kept)
    weight = weight_rows(mine[:vectors], mine[vectors:])
    for step in range(groups):
        first = partner(here, step, groups) * per + ship
        size = 2 * vectors
        for block in range(0, per - ship, 2):
            value = weighted(weight, pair_of(basis, first + block))
            outs[step][block * size : (block + 1) * size, :] = value[:, :LANES]
            outs[step][(block + 1) * size : (block + 2) * size, :] = value[:, LANES:]
        outs[step][(per - ship) * size :, :] = over[...]


def rest_kernel(groups, vectors, kept, ship, scale, over, basis, applied, *refs):
    parts, refs = refs[:groups], refs[groups:]
    pieces, (rest_ref, gram) = refs[:-2], refs[-2:]
    here = lax.axis_index("ba")
    per = basis.shape[0] // groups
    tall = 2 * vectors
    weights = []
    for step in range(groups if ship else 1):
        there = over[...] if step == 0 else parts[step][(per - ship) * tall :, :]
        there = unpacked(there, kept)
        weights.append(weight_rows(there[:vectors], there[vectors:]))
    full = None
    for block in range(0, per, 2):
        mine = here * per + block
        if block < ship:
            total = weighted(weights[0], pair_of(basis, mine))
            for weight, piece in zip(weights[1:], pieces):
                total = total + weighted(weight, row_pairs(piece, block))
        else:
            start = (block - ship) * tall
            total = parts[0][start : start + 2 * tall, :]
            for part in parts[1:]:
                total = total + part[start : start + 2 * tall, :]
            total = jnp.concatenate([total[:tall], total[tall:]], axis=1)
        rest = pair_of(applied, mine) - total
        rest_ref[block] = rest[:, :LANES]
        rest_ref[block + 1] = rest[:, LANES:]
        both = jnp.concatenate(two_halves(rest), axis=0)
        term = lax.dot_general(
            both, both, (((1,), (1,)), ((), ())), preferred_element_type=jnp.float32
        )
        full = term if full is None else full + term
    full = full[: 2 * vectors] + full[2 * vectors :]
    full = full[:, : 2 * vectors] + full[:, 2 * vectors :]
    real, imag = full[:vectors], full[vectors:]
    gram[:, :vectors] = scale * (real[:, :vectors] + imag[:, vectors:])
    gram[:, vectors:] = scale * (real[:, vectors:] - imag[:, :vectors])


def ortho_kernel(groups, vectors, gram, rest, *refs):
    here = lax.axis_index("ba")
    outs, work = refs[:-1], refs[-1]
    shape = (vectors, 2 * vectors)
    row = lax.broadcasted_iota(jnp.int32, shape, 0)
    lane = lax.broadcasted_iota(jnp.int32, shape, 1)
    unit = jnp.where(lane == row + vectors, 1.0, 0.0)
    re = jnp.where(lane < vectors, gram[...], unit)
    im = jnp.concatenate([gram[:, vectors:], jnp.zeros((vectors, vectors), jnp.float32)], axis=1)
    pivots = jnp.ones(shape, jnp.float32)
    for pivot in range(vectors):
        row_re, row_im = re[pivot : pivot + 1], im[pivot : pivot + 1]
        col_re = jnp.broadcast_to(re[:, pivot : pivot + 1], shape)
        col_im = jnp.broadcast_to(im[:, pivot : pivot + 1], shape)
        value = col_re[pivot : pivot + 1]
        inverse = 1.0 / value
        below = row > pivot
        col_re = jnp.where(below, col_re * inverse, 0.0)
        col_im = jnp.where(below, col_im * inverse, 0.0)
        pivots = jnp.where(row == pivot, value, pivots)
        re, im = (
            re - (col_re * row_re - col_im * row_im),
            im - (col_re * row_im + col_im * row_re),
        )
    roots = 1.0 / jnp.sqrt(pivots)
    inv_re, inv_im = (re * roots)[:, vectors:], (im * roots)[:, vectors:]
    own = vectors // groups
    for group in range(groups):
        rows = slice(group * own, (group + 1) * own)
        work[group, :own, :vectors] = inv_re[rows]
        work[group, :own, vectors:] = inv_im[rows]
        work[group, own:, :vectors] = -inv_im[rows]
        work[group, own:, vectors:] = inv_re[rows]
    weight = jnp.concatenate(
        [work[partner(here, step, groups)] for step in range(groups)], axis=0
    )
    high, low = two_halves(weight)
    weight = jnp.concatenate(
        [jnp.concatenate([high, high], axis=1), jnp.concatenate([low, low], axis=1)], axis=0
    )
    for block in range(0, rest.shape[0], 2):
        full = weighted(weight, row_pairs(rest, block))
        for step in range(groups):
            rows = slice(step * 2 * own, (step + 1) * 2 * own)
            outs[step][block] = full[rows, :LANES]
            outs[step][block + 1] = full[rows, LANES:]


def place_kernel(groups, own, rows, *refs):
    parts, out = refs[:groups], refs[groups]
    here = lax.axis_index("ba")
    per = parts[0].shape[0]
    for step in range(groups):
        first = source(here, step, groups) * per
        if per % rows:
            for block in range(per):
                for ri in range(2):
                    out[:, ri, first + block, :] = parts[step][block, ri * own : (ri + 1) * own, :]
        else:
            for block in range(0, per, rows):
                tile = jnp.swapaxes(parts[step][block : block + rows], 0, 1)
                there = pl.ds(pl.multiple_of(first + block, rows), rows)
                for ri in range(2):
                    out[:, ri, there, :] = tile[ri * own : (ri + 1) * own]


def call(kernel, outs, *args, scratch=(), flops=0, grant=6, remote=()):
    nbytes = sum(a.size * a.dtype.itemsize for a in (*args, *outs))
    spec = pl.BlockSpec(memory_space=pltpu.VMEM)
    anywhere = pl.BlockSpec(memory_space=pltpu.HBM)
    return pl.pallas_call(
        kernel,
        out_shape=tuple(outs),
        in_specs=[anywhere if i in remote else spec for i in range(len(args))],
        out_specs=tuple([spec] * len(outs)),
        scratch_shapes=list(scratch),
        compiler_params=pltpu.CompilerParams(vmem_limit_bytes=grant << 20),
        cost_estimate=pl.CostEstimate(flops=flops, bytes_accessed=nbytes, transcendentals=0),
    )(*args)


def shape_of(*dims):
    return jax.ShapeDtypeStruct(dims, jnp.float32)


def tiles_of(value, leading):
    slices, sites = value.shape[-2:]
    value = value.reshape(leading, slices, sites // LANES, LANES)
    return value.swapaxes(1, 2).reshape(leading, slices * sites // LANES, LANES)


def per_device(search_block, kept_basis, gauge_links, clover_term):
    vectors, kept = search_block.shape[0], kept_basis.shape[0]
    slices, sites = search_block.shape[-2:]
    groups, places = lax.axis_size("ba"), lax.axis_size("ta")
    lattice = Lattice(slices, sites)
    rows = lattice.rows
    blocks = COMPS * rows
    per = blocks // groups
    own = vectors // groups
    scale = 1.0 / (2 * COMPS * slices * sites * places)
    psi = tiles_of(search_block, vectors * 2 * COMPS)
    basis = tiles_of(kept_basis, kept * 2 * COMPS).reshape(kept, 2, blocks, LANES)
    ship = per // 4 * 2 if per % rows == 0 else 0
    links = tiles_of(gauge_links, 72)
    clover = tiles_of(clover_term, 144)
    size = vectors // HALVES
    rim = shape_of(size * COMPS // slices, rows, LANES)
    field = shape_of(size * 2 * COMPS, rows, LANES)
    work = size * rows * LANES
    in_hbm = functools.partial(pltpu.with_memory_space_constraint, memory_space=pltpu.HBM)

    def swap(ahead, behind):
        down = [(i, (i + places - 1) % places) for i in range(places)]
        up = [(i, (i + 1) % places) for i in range(places)]
        return lax.ppermute(ahead, "ta", down), lax.ppermute(behind, "ta", up)

    def local(values, base):
        return call(
            functools.partial(local_kernel, lattice, size, base),
            (field,),
            values,
            links,
            clover,
            scratch=[pltpu.VMEM(links.shape, jnp.float32), pltpu.VMEM(clover.shape, jnp.float32)],
            flops=2000 * work,
        )[0]

    opened = call(
        functools.partial(open_kernel, lattice, groups, vectors, kept, ship),
        (rim,) * (2 * HALVES) + (shape_of(max(ship, 1), 2 * kept, LANES),) * (groups - 1),
        in_hbm(psi),
        in_hbm(links),
        in_hbm(basis),
        scratch=[
            pltpu.VMEM(psi.shape, jnp.float32),
            pltpu.VMEM((18, rows, LANES), jnp.float32),
            pltpu.VMEM((groups - 1, kept, 2, -(-ship // rows) * rows or rows, LANES), jnp.float32),
            pltpu.SemaphoreType.DMA((groups + 1,)),
        ],
        flops=400 * work,
        grant=8,
        remote=(0, 1, 2),
    )
    rims = [swap(opened[2 * which], opened[2 * which + 1]) for which in range(HALVES)]
    pieces = exchanged([None, *opened[2 * HALVES :]], "ba")[1:] if ship else []
    parts = []
    for which in range(HALVES):
        part = local(psi, which * size)
        first, ahead, behind = call(
            functools.partial(middle_kernel, lattice, size),
            (field, rim, rim),
            part,
            links,
            *rims[which],
            flops=400 * work,
        )
        rims[which] = swap(ahead, behind)
        parts.append(first)
    (basis_rows,) = call(
        functools.partial(basis_kernel, rows, kept),
        (jax.ShapeDtypeStruct((blocks, 4 * kept, LANES), jnp.bfloat16),),
        basis,
    )
    parts = [local(first, 0) for first in parts]
    applied, over = call(
        functools.partial(correlate_kernel, lattice, vectors, kept, scale),
        (shape_of(blocks, 2 * vectors, LANES), shape_of(2 * vectors * kept // LANES, LANES)),
        *parts,
        links,
        *rims[0],
        basis_rows,
        scratch=[pltpu.VMEM(psi.shape, jnp.float32)],
        flops=400 * work,
    )
    over = summed(over, "ta", (2, 4))
    parts = call(
        functools.partial(project_kernel, groups, vectors, kept, ship),
        (shape_of((per - ship) * 2 * vectors + over.shape[0], LANES),) * groups,
        over,
        basis_rows,
    )
    parts = exchanged(parts, "ba")
    rest, gram = call(
        functools.partial(rest_kernel, groups, vectors, kept, ship, scale),
        (shape_of(per, 2 * vectors, LANES), shape_of(vectors, 2 * vectors)),
        over,
        basis_rows,
        applied,
        *parts,
        *pieces,
    )
    gram = summed(summed(gram, "ta", (2, 4)), "ba", (4,))
    piece = shape_of(per, 2 * own, LANES)
    pieces = call(
        functools.partial(ortho_kernel, groups, vectors),
        (piece,) * groups,
        gram,
        rest,
        scratch=[pltpu.VMEM((groups, 2 * own, 2 * vectors), jnp.float32)],
    )
    pieces = exchanged(pieces, "ba")
    (ortho,) = call(
        functools.partial(place_kernel, groups, own, rows),
        (shape_of(own, 2, blocks, LANES),),
        *pieces,
    )
    ortho = ortho.reshape(own * 2 * COMPS, sites // LANES, slices, LANES).swapaxes(1, 2)
    ortho = ortho.reshape(own, *search_block.shape[1:])
    over = over.reshape(over.shape[0], LANES // kept, kept).swapaxes(0, 1)
    return ortho, over.reshape(2, vectors, kept).swapaxes(1, 2)


def solution(mesh):
    placed = (
        P(None, None, None, None, "ta", None),
        P("ba", None, None, None, "ta", None),
        P(None, None, None, None, "ta", None),
        P(None, None, None, None, "ta", None),
    )


    return jax.shard_map(
        per_device,
        mesh=mesh,
        in_specs=placed,
        out_specs=(P("ba", None, None, None, "ta", None), P(None, "ba", None)),
        check_vma=False,
    )
```

```python
import functools

import jax
import jax.numpy as jnp
from jax import lax
from jax.experimental import pallas as pl
from jax.experimental.pallas import tpu as pltpu
from jax.sharding import PartitionSpec as P


HOPPING = 0.13
LANES = 128
COMPS = 12
PROJECT = (
    ((1, 1), (0, 1)),
    ((1, 0), (0, 2)),
    ((0, 1), (1, 3)),
    ((0, 2), (1, 2)),
)
REBUILD = (
    ((1, 3), (0, 3)),
    ((1, 0), (0, 2)),
    ((0, 3), (1, 1)),
    ((0, 2), (1, 2)),
)


def add_phase(left, right, phase):
    a, b = left
    c, d = right
    phase %= 4
    if phase == 0:
        return a + c, b + d
    if phase == 1:
        return a - d, b + c
    if phase == 2:
        return a - c, b - d
    return a + d, b - c


def plus(left, right):
    return left[0] + right[0], left[1] + right[1]


def minus(left, right):
    return left[0] - right[0], left[1] - right[1]


def rolled(value, shift, axis):
    shift %= value.shape[axis]
    return pltpu.roll(value, shift, axis) if shift else value


class Lattice:
    def __init__(self, slices, sites):
        self.slices = slices
        self.side = round(sites ** (1 / 3))
        self.rows = slices * sites // LANES
        self.shape = (self.rows, LANES)
        if self.side**3 != sites or LANES % (self.side * self.side) or COMPS % slices:
            raise ValueError("lattice shape")

    def masks(self):
        lane = lax.broadcasted_iota(jnp.int32, self.shape, 1)
        row = lax.broadcasted_iota(jnp.int32, self.shape, 0)
        side = self.side
        self.time = row % self.slices
        self.x_low = lane // (side * side)
        self.y = lane // side % side
        self.z = lane % side

    def shift(self, value, direction, ahead):
        side, area = self.side, self.side * self.side
        if direction == 0:
            step = 1 if ahead else -1
            edge = self.x_low == (0 if ahead else LANES // area - 1)
            mixed = jnp.where(edge, rolled(value, -step * self.slices, 0), value)
            return rolled(mixed, -step * area, 1)
        if direction < 3:
            place, unit = (self.y, side) if direction == 1 else (self.z, 1)
            edge = place == (side - 1 if ahead else 0)
            step = unit if ahead else -unit
            return jnp.where(
                edge, rolled(value, (side - 1) * step, 1), rolled(value, -step, 1)
            )
        if ahead:
            return jnp.where(self.time == self.slices - 1, 0.0, rolled(value, -1, 0))
        return jnp.where(self.time == 0, 0.0, rolled(value, 1, 0))


def load_spinor(ref, vector):
    def at(spin, colour):
        place = vector * (2 * COMPS) + spin * 3 + colour
        return ref[place], ref[place + COMPS]

    return at


def link_at(links, direction):
    def at(row, column):
        place = direction * 18 + row * 3 + column
        u, v = links[place], links[place + 9]
        return u, v + u, v - u

    return at


def entry_sums(values, size, sums):
    for matrix in range(values.shape[0] // (2 * size)):
        for entry in range(size):
            u = values[matrix * 2 * size + entry]
            v = values[matrix * 2 * size + size + entry]
            sums[matrix * 2 * size + entry] = v + u
            sums[matrix * 2 * size + size + entry] = v - u


def summed_link_at(links, sums, direction):
    def at(row, column):
        place = direction * 18 + row * 3 + column
        return links[place], sums[place], sums[place + 9]

    return at


def sums_of(halves):
    return [[(a, b, a + b) for a, b in half] for half in halves]


def times_link(link, halves):
    out = [[None] * 3 for _ in halves]
    for row in range(3):
        totals = [None] * len(halves)
        for column in range(3):
            u, s, d = link(row, column)
            for which, half in enumerate(halves):
                a, b, ab = half[column]
                terms = (u * ab, s * b, d * a)
                old = totals[which]
                totals[which] = terms if old is None else [x + y for x, y in zip(old, terms)]
        for which, (both, re, im) in enumerate(totals):
            out[which][row] = (both - re, both + im)
    return out


def times_dagger(link, halves):
    out = [[None] * 3 for _ in halves]
    for row in range(3):
        totals = [None] * len(halves)
        for column in range(3):
            u, s, d = link(column, row)
            for which, half in enumerate(halves):
                a, b, ab = half[column]
                terms = (u * ab, d * b, s * a)
                old = totals[which]
                totals[which] = terms if old is None else [x + y for x, y in zip(old, terms)]
        for which, (both, re, im) in enumerate(totals):
            out[which][row] = (both + re, both - im)
    return out


def half_spinor(spinor, direction, spin, ahead):
    other, phase = PROJECT[direction][spin]
    phase = phase if ahead else phase + 2
    return [add_phase(spinor(spin, c), spinor(2 + other, c), phase) for c in range(3)]


def pack_rim(lattice, spinor, links, ahead_ref, behind_ref, vector):
    slices = lattice.slices
    ahead = half_spinor(spinor, 3, 0, True) + half_spinor(spinor, 3, 1, True)
    halves = [half_spinor(spinor, 3, spin, False) for spin in range(2)]
    behind = times_dagger(link_at(links, 3), sums_of(halves))
    behind = behind[0] + behind[1]
    for values, origin, ref in ((ahead, 0, ahead_ref), (behind, slices - 1, behind_ref)):
        flat = [part for pair in values for part in pair]
        for group in range(COMPS // slices):
            tile = None
            for place in range(slices):
                moved = rolled(flat[group * slices + place], place - origin, 0)
                tile = moved if tile is None else jnp.where(lattice.time == place, moved, tile)
            ref[vector * (COMPS // slices) + group] = tile


def unpack_rim(lattice, ref, vector, ahead, sign):
    slices = lattice.slices
    target = slices - 1 if ahead else 0
    flat = []
    for comp in range(COMPS):
        tile = ref[vector * (COMPS // slices) + comp // slices]
        moved = rolled(tile, target - comp % slices, 0)
        flat.append(jnp.where(lattice.time == target, moved * sign, 0.0))
    return [(flat[2 * i], flat[2 * i + 1]) for i in range(COMPS // 2)]


def open_kernel(
    lattice, groups, vectors, kept, ship,
    psi_ref, links_ref, basis, *refs,
):
    psi, links, ahead_ref, behind_ref = refs[:4]
    pieces = refs[4 : groups + 3]
    held, sems = refs[groups + 3 :]
    here = lax.axis_index("ba")
    rows, per = lattice.rows, basis.shape[2] // groups
    fields = pltpu.make_async_copy(psi_ref, psi, sems.at[0])
    links_in = pltpu.make_async_copy(links_ref, links, sems.at[1])
    kept_in = []
    for step in range(1, groups if ship else 1):
        start = pl.multiple_of(partner(here, step, groups) * per, rows)
        kept_in.append(
            pltpu.make_async_copy(
                basis.at[:, :, pl.ds(start, held.shape[3]), :], held.at[step - 1], sems.at[1 + step]
            )
        )
    for copy in (links_in, fields, *kept_in):
        copy.start()
    lattice.masks()
    links_in.wait()
    fields.wait()

    def body(vector, carry):
        pack_rim(lattice, load_spinor(psi, vector), links, ahead_ref, behind_ref, vector)
        return carry

    lax.fori_loop(0, vectors, body, 0, unroll=2)
    for step, copy in enumerate(kept_in):
        copy.wait()

        def turn(group, carry, step=step):
            first = pl.multiple_of(group * 8, 8)
            for ri in range(2):
                for start in range(0, ship, rows):
                    tile = held[step, pl.ds(first, 8), ri, start : start + rows, :]
                    tile = jnp.swapaxes(tile, 0, 1)
                    size = min(rows, ship - start)
                    pieces[step][start : start + size, pl.ds(ri * kept + first, 8), :] = tile[:size]
            return carry

        lax.fori_loop(0, kept // 8, turn, 0)


def basis_kernel(rows, kept, basis, out):
    def body(tile, carry):
        blocks = pl.ds(pl.multiple_of(tile * rows, rows), rows)
        for ri in range(2):
            for first in range(0, kept, 16):
                value = jnp.swapaxes(basis[first : first + 16, ri, blocks, :], 0, 1)
                high, low = two_halves(value)
                start = ri * kept + first
                out[blocks, start : start + 16, :] = high
                out[blocks, 2 * kept + start : 2 * kept + start + 16, :] = low
        return carry

    lax.fori_loop(0, basis.shape[2] // rows, body, 0)


def local_kernel(lattice, vectors, psi, links, clover, out, link_sums, clover_sums):
    lattice.masks()
    entry_sums(links, 9, link_sums)
    entry_sums(clover, 36, clover_sums)

    def body(vector, carry):
        spinor = load_spinor(psi, vector)
        upper = [[None] * 3 for _ in range(2)]
        lower = [[None] * 3 for _ in range(2)]
        for direction in range(4):
            link = summed_link_at(links, link_sums, direction)
            halves = []
            for spin in range(2):
                half = half_spinor(spinor, direction, spin, True)
                halves.append([tuple(lattice.shift(p, direction, True) for p in h) for h in half])
            aheads = times_link(link, sums_of(halves))
            halves = [half_spinor(spinor, direction, spin, False) for spin in range(2)]
            behinds = times_dagger(link, sums_of(halves))
            for spin in range(2):
                ahead = aheads[spin]
                behind = [
                    tuple(lattice.shift(p, direction, False) for p in h) for h in behinds[spin]
                ]
                place, phase = REBUILD[direction][spin]
                for c in range(3):
                    total, diff = plus(ahead[c], behind[c]), minus(ahead[c], behind[c])
                    if upper[spin][c] is None:
                        upper[spin][c] = total
                    else:
                        upper[spin][c] = plus(upper[spin][c], total)
                    if lower[place][c] is None:
                        zero = jnp.zeros_like(diff[0])
                        lower[place][c] = add_phase((zero, zero), diff, phase)
                    else:
                        lower[place][c] = add_phase(lower[place][c], diff, phase)
        for chiral, hops in ((0, upper), (1, lower)):
            field = [spinor(2 * chiral + i // 3, i % 3) for i in range(6)]
            field = [(x, y, x + y) for x, y in field]
            for row in range(6):
                total = None
                for column in range(6):
                    place = chiral * 72 + row * 6 + column
                    a, b, ab = field[column]
                    terms = (
                        clover[place] * ab,
                        clover_sums[place] * b,
                        clover_sums[place + 36] * a,
                    )
                    total = terms if total is None else [x + y for x, y in zip(total, terms)]
                both, re, im = total
                place = vector * (2 * COMPS) + chiral * 6 + row
                out[place] = both - re - HOPPING * hops[row // 3][row % 3][0]
                out[place + COMPS] = both + im - HOPPING * hops[row // 3][row % 3][1]
        return carry

    lax.fori_loop(0, vectors, body, 0)


def rim_signs():
    count, here = lax.axis_size("ta"), lax.axis_index("ta")
    one = jnp.float32(1.0)
    return jnp.where(here == count - 1, -one, one), jnp.where(here == 0, -one, one)


def finish(lattice, links, part, rim_ahead, rim_behind, vector, signs, store):
    ahead_all = unpack_rim(lattice, rim_ahead, vector, True, signs[0])
    behind_all = unpack_rim(lattice, rim_behind, vector, False, signs[1])
    both = times_link(link_at(links, 3), sums_of([ahead_all[:3], ahead_all[3:]]))
    for spin in range(2):
        ahead = both[spin]
        behind = behind_all[3 * spin : 3 * spin + 3]
        for c in range(3):
            for ri in range(2):
                f, b = ahead[c][ri], behind[c][ri]
                place = vector * (2 * COMPS) + ri * COMPS + spin * 3 + c
                store(place, part[place] - HOPPING * (f + b))
                store(place + 6, -(part[place + 6] + HOPPING * (f - b)))


def middle_kernel(
    lattice, vectors, part, links, rim_ahead, rim_behind, out, ahead_ref, behind_ref
):
    lattice.masks()
    signs = rim_signs()

    def body(vector, carry):
        def store(place, value):
            out[place] = value

        finish(lattice, links, part, rim_ahead, rim_behind, vector, signs, store)
        pack_rim(lattice, load_spinor(out, vector), links, ahead_ref, behind_ref, vector)
        return carry

    lax.fori_loop(0, vectors, body, 0)


def two_halves(value):
    high = value.astype(jnp.bfloat16)
    return high, (value - high.astype(jnp.float32)).astype(jnp.bfloat16)


def spans(first, last):
    return [(i, min(2, last - i)) for i in range(first, last, 2)]


def beside(ref, block, count):
    return jnp.concatenate([ref[block + i] for i in range(count)], axis=1)


def halves_beside(ref, block, count):
    return jnp.concatenate(two_halves(beside(ref, block, count)), axis=0)


def correlate_kernel(
    lattice, size, kept, scale, part, links, rim_ahead, rim_behind, basis, applied, over, field,
):
    lattice.masks()
    signs = rim_signs()
    rows = lattice.rows

    def body(vector, carry):
        def store(place, value):
            field[place] = value

        finish(lattice, links, part, rim_ahead, rim_behind, vector, signs, store)
        return carry

    lax.fori_loop(0, size, body, 0, unroll=2)

    total = jnp.zeros((4 * size, 4 * kept), jnp.float32)
    for comp in range(COMPS):
        blocks_here = slice(comp * rows, (comp + 1) * rows)
        for ri in range(2):
            for first in range(0, size, 8):
                count = min(8, size - first)
                tiles = jnp.stack(
                    [field[(first + i) * 2 * COMPS + ri * COMPS + comp] for i in range(count)]
                )
                start = ri * size + first
                applied[blocks_here, start : start + count, :] = jnp.swapaxes(tiles, 0, 1)
        mine = jnp.concatenate([applied[comp * rows + i] for i in range(rows)], axis=1)
        kept_rows = jnp.concatenate([basis[comp * rows + i] for i in range(rows)], axis=1)
        total = total + lax.dot_general(
            jnp.concatenate(two_halves(mine), axis=0),
            kept_rows,
            (((1,), (1,)), ((), ())),
            preferred_element_type=jnp.float32,
        )
    total = total[: 2 * size] + total[2 * size :]
    total = total[:, : 2 * kept] + total[:, 2 * kept :]
    real, imag = total[:size], total[size:]
    real, imag = (
        scale * (real[:, :kept] + imag[:, kept:]),
        scale * (imag[:, :kept] - real[:, kept:]),
    )
    over[...] = packed(jnp.concatenate([real, imag], axis=0))


def partner(here, step, count):
    if count & (count - 1) == 0:
        return here ^ step
    return (here + step) % count


def source(here, step, count):
    if count & (count - 1) == 0:
        return here ^ step
    return (here + count - step) % count


def exchanged(values, axis):
    count = lax.axis_size(axis)
    out = [values[0]]
    for step in range(1, count):
        pairs = [(i, partner(i, step, count)) for i in range(count)]
        out.append(lax.ppermute(values[step], axis, pairs))
    return out


def summed(value, axis, radix):
    count = lax.axis_size(axis)
    if count & (count - 1):
        return lax.psum(value, axis)
    stride = 1
    while stride < count:
        size, radix = min(radix[0], count // stride), radix[1:] or radix
        total = value
        for step in range(1, size):
            moved = lax.ppermute(value, axis, [(i, i ^ (step * stride)) for i in range(count)])
            total = total + moved
        value = total
        stride *= size
    return value


def packed(value):
    count = LANES // value.shape[1]
    size = value.shape[0] // count
    return jnp.concatenate([value[i * size : (i + 1) * size] for i in range(count)], axis=1)


def unpacked(value, width):
    return jnp.concatenate(
        [value[:, i * width : (i + 1) * width] for i in range(LANES // width)], axis=0
    )


def weight_rows(real, imag):
    weight = jnp.concatenate(
        [jnp.concatenate([real, -imag], axis=1), jnp.concatenate([imag, real], axis=1)], axis=0
    )
    high, low = two_halves(weight)
    return jnp.concatenate(
        [jnp.concatenate([high, high], axis=1), jnp.concatenate([low, low], axis=1)], axis=0
    )


def weighted(weight, basis):
    both = jnp.dot(weight, basis, preferred_element_type=jnp.float32)
    half = both.shape[0] // 2
    return both[:half] + both[half:]


def project_kernel(groups, vectors, kept, ship, over, basis, *outs):
    here = lax.axis_index("ba")
    per = basis.shape[0] // groups
    mine = unpacked(over[...], kept)
    weight = weight_rows(mine[:vectors], mine[vectors:])
    size = 2 * vectors
    for step in range(groups):
        first = partner(here, step, groups) * per + ship
        for block, count in spans(0, per - ship):
            value = weighted(weight, beside(basis, first + block, count))
            for i in range(count):
                start = (block + i) * size
                outs[step][start : start + size, :] = value[:, i * LANES : (i + 1) * LANES]
        outs[step][(per - ship) * size :, :] = over[...]


def rest_kernel(groups, vectors, kept, ship, scale, over, basis, applied, *refs):
    parts, refs = refs[:groups], refs[groups:]
    pieces, (rest_ref, gram) = refs[:-2], refs[-2:]
    here = lax.axis_index("ba")
    per = basis.shape[0] // groups
    tall = 2 * vectors
    weights = []
    for step in range(groups if ship else 1):
        there = over[...] if step == 0 else parts[step][(per - ship) * tall :, :]
        there = unpacked(there, kept)
        weights.append(weight_rows(there[:vectors], there[vectors:]))
    full = None
    for block, count in spans(0, ship) + spans(ship, per):
        mine = here * per + block
        if block < ship:
            total = weighted(weights[0], beside(basis, mine, count))
            for weight, piece in zip(weights[1:], pieces):
                total = total + weighted(weight, halves_beside(piece, block, count))
        else:
            here_rows = slice((block - ship) * tall, (block - ship + count) * tall)
            total = parts[0][here_rows, :]
            for part in parts[1:]:
                total = total + part[here_rows, :]
            total = jnp.concatenate(
                [total[i * tall : (i + 1) * tall] for i in range(count)], axis=1
            )
        rest = beside(applied, mine, count) - total
        for i in range(count):
            rest_ref[block + i] = rest[:, i * LANES : (i + 1) * LANES]
        both = jnp.concatenate(two_halves(rest), axis=0)
        term = lax.dot_general(
            both, both, (((1,), (1,)), ((), ())), preferred_element_type=jnp.float32
        )
        full = term if full is None else full + term
    full = full[: 2 * vectors] + full[2 * vectors :]
    full = full[:, : 2 * vectors] + full[:, 2 * vectors :]
    real, imag = full[:vectors], full[vectors:]
    gram[:, :vectors] = scale * (real[:, :vectors] + imag[:, vectors:])
    gram[:, vectors:] = scale * (real[:, vectors:] - imag[:, :vectors])


def ortho_kernel(groups, vectors, gram, rest, *refs):
    here = lax.axis_index("ba")
    outs, work = refs[:-1], refs[-1]
    shape = (vectors, 2 * vectors)
    row = lax.broadcasted_iota(jnp.int32, shape, 0)
    lane = lax.broadcasted_iota(jnp.int32, shape, 1)
    unit = jnp.where(lane == row + vectors, 1.0, 0.0)
    re = jnp.where(lane < vectors, gram[...], unit)
    im = jnp.concatenate([gram[:, vectors:], jnp.zeros((vectors, vectors), jnp.float32)], axis=1)
    pivots = jnp.ones(shape, jnp.float32)
    link_re = link_im = jnp.zeros(shape, jnp.float32)
    for first in range(0, vectors, 2):
        second = first + 1
        row0 = re[first:second], im[first:second]
        row1 = re[second : second + 1], im[second : second + 1]
        x0 = [jnp.broadcast_to(x[:, first:second], shape) for x in (re, im)]
        x1 = [jnp.broadcast_to(x[:, second : second + 1], shape) for x in (re, im)]
        top, low = x0[0][first:second], x1[0][second : second + 1]
        b_re, b_im = x1[0][first:second], x1[1][first:second]
        square = b_re * b_re + b_im * b_im
        inverse = jnp.where(row > second, 1.0 / (top * low - square), 0.0)
        f0_re = (x0[0] * low - (x1[0] * b_re + x1[1] * b_im)) * inverse
        f0_im = (x0[1] * low - (x1[1] * b_re - x1[0] * b_im)) * inverse
        f1_re = (x1[0] * top - (x0[0] * b_re - x0[1] * b_im)) * inverse
        f1_im = (x1[1] * top - (x0[0] * b_im + x0[1] * b_re)) * inverse
        here_first, here_second = row == first, row == second
        share = 1.0 / top
        pivots = jnp.where(
            here_first, top, jnp.where(here_second, low - square * share, pivots)
        )
        link_re = jnp.where(here_second, b_re * share, link_re)
        link_im = jnp.where(here_second, -b_im * share, link_im)
        re, im = (
            re - ((f0_re * row0[0] - f0_im * row0[1]) + (f1_re * row1[0] - f1_im * row1[1])),
            im - ((f0_re * row0[1] + f0_im * row0[0]) + (f1_re * row1[1] + f1_im * row1[0])),
        )
    above_re, above_im = pltpu.roll(re, 1, 0), pltpu.roll(im, 1, 0)
    re, im = (
        re - (link_re * above_re - link_im * above_im),
        im - (link_re * above_im + link_im * above_re),
    )
    roots = 1.0 / jnp.sqrt(pivots)
    inv_re, inv_im = (re * roots)[:, vectors:], (im * roots)[:, vectors:]
    own = vectors // groups
    for group in range(groups):
        rows = slice(group * own, (group + 1) * own)
        work[group, :own, :vectors] = inv_re[rows]
        work[group, :own, vectors:] = inv_im[rows]
        work[group, own:, :vectors] = -inv_im[rows]
        work[group, own:, vectors:] = inv_re[rows]
    weight = jnp.concatenate(
        [work[partner(here, step, groups)] for step in range(groups)], axis=0
    )
    high, low = two_halves(weight)
    weight = jnp.concatenate(
        [jnp.concatenate([high, high], axis=1), jnp.concatenate([low, low], axis=1)], axis=0
    )
    for block, count in spans(0, rest.shape[0]):
        full = weighted(weight, halves_beside(rest, block, count))
        for step in range(groups):
            rows = slice(step * 2 * own, (step + 1) * 2 * own)
            for i in range(count):
                outs[step][block + i] = full[rows, i * LANES : (i + 1) * LANES]


def place_kernel(groups, own, rows, *refs):
    parts, out = refs[:groups], refs[groups]
    here = lax.axis_index("ba")
    per = parts[0].shape[0]
    for step in range(groups):
        first = source(here, step, groups) * per
        if per % rows:
            for block in range(per):
                for ri in range(2):
                    out[:, ri, first + block, :] = parts[step][block, ri * own : (ri + 1) * own, :]
        else:
            for block in range(0, per, rows):
                tile = jnp.swapaxes(parts[step][block : block + rows], 0, 1)
                there = pl.ds(pl.multiple_of(first + block, rows), rows)
                for ri in range(2):
                    out[:, ri, there, :] = tile[ri * own : (ri + 1) * own]


def call(kernel, outs, *args, scratch=(), flops=0, grant=6, remote=()):
    nbytes = sum(a.size * a.dtype.itemsize for a in (*args, *outs))
    spec = pl.BlockSpec(memory_space=pltpu.VMEM)
    anywhere = pl.BlockSpec(memory_space=pltpu.HBM)
    return pl.pallas_call(
        kernel,
        out_shape=tuple(outs),
        in_specs=[anywhere if i in remote else spec for i in range(len(args))],
        out_specs=tuple([spec] * len(outs)),
        scratch_shapes=list(scratch),
        compiler_params=pltpu.CompilerParams(vmem_limit_bytes=grant << 20),
        cost_estimate=pl.CostEstimate(flops=flops, bytes_accessed=nbytes, transcendentals=0),
    )(*args)


def shape_of(*dims):
    return jax.ShapeDtypeStruct(dims, jnp.float32)


def tiles_of(value, leading):
    slices, sites = value.shape[-2:]
    value = value.reshape(leading, slices, sites // LANES, LANES)
    return value.swapaxes(1, 2).reshape(leading, slices * sites // LANES, LANES)


def per_device(search_block, kept_basis, gauge_links, clover_term):
    vectors, kept = search_block.shape[0], kept_basis.shape[0]
    slices, sites = search_block.shape[-2:]
    groups, places = lax.axis_size("ba"), lax.axis_size("ta")
    lattice = Lattice(slices, sites)
    rows = lattice.rows
    blocks = COMPS * rows
    per = blocks // groups
    own = vectors // groups
    scale = 1.0 / (2 * COMPS * slices * sites * places)
    psi = tiles_of(search_block, vectors * 2 * COMPS)
    basis = tiles_of(kept_basis, kept * 2 * COMPS).reshape(kept, 2, blocks, LANES)
    ship = per * 11 // 24 if per % rows == 0 else 0
    links = tiles_of(gauge_links, 72)
    clover = tiles_of(clover_term, 144)
    rim = shape_of(vectors * COMPS // slices, rows, LANES)
    field = shape_of(vectors * 2 * COMPS, rows, LANES)
    work = vectors * rows * LANES
    in_hbm = functools.partial(pltpu.with_memory_space_constraint, memory_space=pltpu.HBM)

    def swap(ahead, behind):
        down = [(i, (i + places - 1) % places) for i in range(places)]
        up = [(i, (i + 1) % places) for i in range(places)]
        return lax.ppermute(ahead, "ta", down), lax.ppermute(behind, "ta", up)

    def local(values):
        return call(
            functools.partial(local_kernel, lattice, vectors),
            (field,),
            values,
            links,
            clover,
            scratch=[pltpu.VMEM(links.shape, jnp.float32), pltpu.VMEM(clover.shape, jnp.float32)],
            flops=2000 * work,
        )[0]

    psi, links, ahead, behind, *pieces = call(
        functools.partial(open_kernel, lattice, groups, vectors, kept, ship),
        (field, shape_of(*links.shape), rim, rim)
        + (shape_of(max(ship, 1), 2 * kept, LANES),) * (groups - 1),
        in_hbm(psi),
        in_hbm(links),
        in_hbm(basis),
        scratch=[
            pltpu.VMEM((groups - 1, kept, 2, -(-ship // rows) * rows or rows, LANES), jnp.float32),
            pltpu.SemaphoreType.DMA((groups + 1,)),
        ],
        flops=400 * work,
        grant=8,
        remote=(0, 1, 2),
    )
    rims = swap(ahead, behind)
    pieces = exchanged([None, *pieces], "ba")[1:] if ship else []
    part = local(psi)
    first, ahead, behind = call(
        functools.partial(middle_kernel, lattice, vectors),
        (field, rim, rim),
        part,
        links,
        *rims,
        flops=400 * work,
    )
    rims = swap(ahead, behind)
    (basis_rows,) = call(
        functools.partial(basis_kernel, rows, kept),
        (jax.ShapeDtypeStruct((blocks, 4 * kept, LANES), jnp.bfloat16),),
        basis,
    )
    part = local(first)
    applied, over = call(
        functools.partial(correlate_kernel, lattice, vectors, kept, scale),
        (shape_of(blocks, 2 * vectors, LANES), shape_of(2 * vectors * kept // LANES, LANES)),
        part,
        links,
        *rims,
        basis_rows,
        scratch=[pltpu.VMEM(psi.shape, jnp.float32)],
        flops=400 * work,
    )
    over = summed(over, "ta", (2, 4))
    parts = call(
        functools.partial(project_kernel, groups, vectors, kept, ship),
        (shape_of((per - ship) * 2 * vectors + over.shape[0], LANES),) * groups,
        over,
        basis_rows,
    )
    parts = exchanged(parts, "ba")
    rest, gram = call(
        functools.partial(rest_kernel, groups, vectors, kept, ship, scale),
        (shape_of(per, 2 * vectors, LANES), shape_of(vectors, 2 * vectors)),
        over,
        basis_rows,
        applied,
        *parts,
        *pieces,
    )
    gram = summed(gram, "ta", (2, 4))
    gram = summed(gram, "ba", (4,))
    piece = shape_of(per, 2 * own, LANES)
    pieces = call(
        functools.partial(ortho_kernel, groups, vectors),
        (piece,) * groups,
        gram,
        rest,
        scratch=[pltpu.VMEM((groups, 2 * own, 2 * vectors), jnp.float32)],
    )
    pieces = exchanged(pieces, "ba")
    (ortho,) = call(
        functools.partial(place_kernel, groups, own, rows),
        (shape_of(own, 2, blocks, LANES),),
        *pieces,
    )
    ortho = ortho.reshape(own * 2 * COMPS, sites // LANES, slices, LANES).swapaxes(1, 2)
    ortho = ortho.reshape(own, *search_block.shape[1:])
    over = over.reshape(over.shape[0], LANES // kept, kept).swapaxes(0, 1)
    return ortho, over.reshape(2, vectors, kept).swapaxes(1, 2)


def solution(mesh):
    placed = (
        P(None, None, None, None, "ta", None),
        P("ba", None, None, None, "ta", None),
        P(None, None, None, None, "ta", None),
        P(None, None, None, None, "ta", None),
    )


    return jax.shard_map(
        per_device,
        mesh=mesh,
        in_specs=placed,
        out_specs=(P("ba", None, None, None, "ta", None), P(None, "ba", None)),
        check_vma=False,
    )
```

```python
import functools

import jax
import jax.numpy as jnp
from jax import lax
from jax.experimental import pallas as pl
from jax.experimental.pallas import tpu as pltpu
from jax.sharding import PartitionSpec as P


HOPPING = 0.13
LANES = 128
CHUNKS = 4
COMPS = 12
PROJECT = (
    ((1, 1), (0, 1)),
    ((1, 0), (0, 2)),
    ((0, 1), (1, 3)),
    ((0, 2), (1, 2)),
)
REBUILD = (
    ((1, 3), (0, 3)),
    ((1, 0), (0, 2)),
    ((0, 3), (1, 1)),
    ((0, 2), (1, 2)),
)


def add_phase(left, right, phase):
    a, b = left
    c, d = right
    phase %= 4
    if phase == 0:
        return a + c, b + d
    if phase == 1:
        return a - d, b + c
    if phase == 2:
        return a - c, b - d
    return a + d, b - c


def plus(left, right):
    return left[0] + right[0], left[1] + right[1]


def minus(left, right):
    return left[0] - right[0], left[1] - right[1]


def rolled(value, shift, axis):
    shift %= value.shape[axis]
    return pltpu.roll(value, shift, axis) if shift else value


class Lattice:
    def __init__(self, slices, sites):
        self.slices = slices
        self.side = round(sites ** (1 / 3))
        self.rows = slices * sites // LANES
        self.shape = (self.rows, LANES)
        if self.side**3 != sites or LANES % (self.side * self.side) or COMPS % slices:
            raise ValueError("lattice shape")

    def masks(self):
        lane = lax.broadcasted_iota(jnp.int32, self.shape, 1)
        row = lax.broadcasted_iota(jnp.int32, self.shape, 0)
        side = self.side
        self.time = row % self.slices
        self.x_low = lane // (side * side)
        self.y = lane // side % side
        self.z = lane % side

    def shift(self, value, direction, ahead):
        side, area = self.side, self.side * self.side
        if direction == 0:
            step = 1 if ahead else -1
            edge = self.x_low == (0 if ahead else LANES // area - 1)
            mixed = jnp.where(edge, rolled(value, -step * self.slices, 0), value)
            return rolled(mixed, -step * area, 1)
        if direction < 3:
            place, unit = (self.y, side) if direction == 1 else (self.z, 1)
            edge = place == (side - 1 if ahead else 0)
            step = unit if ahead else -unit
            return jnp.where(
                edge, rolled(value, (side - 1) * step, 1), rolled(value, -step, 1)
            )
        if ahead:
            return jnp.where(self.time == self.slices - 1, 0.0, rolled(value, -1, 0))
        return jnp.where(self.time == 0, 0.0, rolled(value, 1, 0))


def load_spinor(ref, vector):
    def at(spin, colour):
        place = vector * (2 * COMPS) + spin * 3 + colour
        return ref[place], ref[place + COMPS]

    return at


def link_at(links, direction):
    def at(row, column):
        place = direction * 18 + row * 3 + column
        u, v = links[place], links[place + 9]
        return u, v + u, v - u

    return at


def entry_sums(values, size, sums):
    for matrix in range(values.shape[0] // (2 * size)):
        for entry in range(size):
            u = values[matrix * 2 * size + entry]
            v = values[matrix * 2 * size + size + entry]
            sums[matrix * 2 * size + entry] = v + u
            sums[matrix * 2 * size + size + entry] = v - u


def summed_link_at(links, sums, direction):
    def at(row, column):
        place = direction * 18 + row * 3 + column
        return links[place], sums[place], sums[place + 9]

    return at


def sums_of(halves):
    return [[(a, b, a + b) for a, b in half] for half in halves]


def times_link(link, halves):
    out = [[None] * 3 for _ in halves]
    for row in range(3):
        totals = [None] * len(halves)
        for column in range(3):
            u, s, d = link(row, column)
            for which, half in enumerate(halves):
                a, b, ab = half[column]
                terms = (u * ab, s * b, d * a)
                old = totals[which]
                totals[which] = terms if old is None else [x + y for x, y in zip(old, terms)]
        for which, (both, re, im) in enumerate(totals):
            out[which][row] = (both - re, both + im)
    return out


def times_dagger(link, halves):
    out = [[None] * 3 for _ in halves]
    for row in range(3):
        totals = [None] * len(halves)
        for column in range(3):
            u, s, d = link(column, row)
            for which, half in enumerate(halves):
                a, b, ab = half[column]
                terms = (u * ab, d * b, s * a)
                old = totals[which]
                totals[which] = terms if old is None else [x + y for x, y in zip(old, terms)]
        for which, (both, re, im) in enumerate(totals):
            out[which][row] = (both + re, both - im)
    return out


def half_spinor(spinor, direction, spin, ahead):
    other, phase = PROJECT[direction][spin]
    phase = phase if ahead else phase + 2
    return [add_phase(spinor(spin, c), spinor(2 + other, c), phase) for c in range(3)]


def pack_rim(lattice, spinor, links, ahead_ref, behind_ref, vector):
    slices = lattice.slices
    ahead = half_spinor(spinor, 3, 0, True) + half_spinor(spinor, 3, 1, True)
    halves = [half_spinor(spinor, 3, spin, False) for spin in range(2)]
    behind = times_dagger(link_at(links, 3), sums_of(halves))
    behind = behind[0] + behind[1]
    for values, origin, ref in ((ahead, 0, ahead_ref), (behind, slices - 1, behind_ref)):
        flat = [part for pair in values for part in pair]
        for group in range(COMPS // slices):
            tile = None
            for place in range(slices):
                moved = rolled(flat[group * slices + place], place - origin, 0)
                tile = moved if tile is None else jnp.where(lattice.time == place, moved, tile)
            ref[vector * (COMPS // slices) + group] = tile


def unpack_rim(lattice, ref, vector, ahead, sign):
    slices = lattice.slices
    target = slices - 1 if ahead else 0
    flat = []
    for comp in range(COMPS):
        tile = ref[vector * (COMPS // slices) + comp // slices]
        moved = rolled(tile, target - comp % slices, 0)
        flat.append(jnp.where(lattice.time == target, moved * sign, 0.0))
    return [(flat[2 * i], flat[2 * i + 1]) for i in range(COMPS // 2)]


def open_kernel(
    lattice, groups, vectors, kept, ship,
    psi_ref, links_ref, basis, *refs,
):
    psi, links, ahead_ref, behind_ref = refs[:4]
    pieces = refs[4 : groups + 3]
    held, sems = refs[groups + 3 :]
    here = lax.axis_index("ba")
    rows, per = lattice.rows, basis.shape[2] // groups
    vectors_each = vectors // CHUNKS if vectors % CHUNKS == 0 else vectors
    chunks = vectors // vectors_each
    size = vectors_each * 2 * COMPS
    fields = [
        pltpu.make_async_copy(
            psi_ref.at[pl.ds(i * size, size)], psi.at[pl.ds(i * size, size)], sems.at[groups + i]
        )
        for i in range(chunks)
    ]
    links_in = pltpu.make_async_copy(links_ref, links, sems.at[0])
    kept_in = []
    for step in range(1, groups if ship else 1):
        start = pl.multiple_of(partner(here, step, groups) * per, rows)
        kept_in.append(
            pltpu.make_async_copy(
                basis.at[:, :, pl.ds(start, held.shape[3]), :], held.at[step - 1], sems.at[step]
            )
        )
    for copy in (links_in, *fields, *kept_in):
        copy.start()
    lattice.masks()
    links_in.wait()

    def body(vector, carry):
        pack_rim(lattice, load_spinor(psi, vector), links, ahead_ref, behind_ref, vector)
        return carry

    for i, copy in enumerate(fields):
        copy.wait()
        lax.fori_loop(i * vectors_each, (i + 1) * vectors_each, body, 0, unroll=2)
    for step, copy in enumerate(kept_in):
        copy.wait()

        def turn(group, carry, step=step):
            first = pl.multiple_of(group * 8, 8)
            for ri in range(2):
                for start in range(0, ship, rows):
                    tile = held[step, pl.ds(first, 8), ri, start : start + rows, :]
                    tile = jnp.swapaxes(tile, 0, 1)
                    size = min(rows, ship - start)
                    pieces[step][start : start + size, pl.ds(ri * kept + first, 8), :] = tile[:size]
            return carry

        lax.fori_loop(0, kept // 8, turn, 0)


def basis_kernel(rows, kept, basis, out):
    def body(tile, carry):
        blocks = pl.ds(pl.multiple_of(tile * rows, rows), rows)
        for ri in range(2):
            for first in range(0, kept, 16):
                value = jnp.swapaxes(basis[first : first + 16, ri, blocks, :], 0, 1)
                high, low = two_halves(value)
                start = ri * kept + first
                out[blocks, start : start + 16, :] = high
                out[blocks, 2 * kept + start : 2 * kept + start + 16, :] = low
        return carry

    lax.fori_loop(0, basis.shape[2] // rows, body, 0)


def local_kernel(lattice, vectors, psi, links, clover, out, link_sums, clover_sums):
    lattice.masks()
    entry_sums(links, 9, link_sums)
    entry_sums(clover, 36, clover_sums)

    def body(vector, carry):
        spinor = load_spinor(psi, vector)
        upper = [[None] * 3 for _ in range(2)]
        lower = [[None] * 3 for _ in range(2)]
        for direction in range(4):
            link = summed_link_at(links, link_sums, direction)
            halves = []
            for spin in range(2):
                half = half_spinor(spinor, direction, spin, True)
                halves.append([tuple(lattice.shift(p, direction, True) for p in h) for h in half])
            aheads = times_link(link, sums_of(halves))
            halves = [half_spinor(spinor, direction, spin, False) for spin in range(2)]
            behinds = times_dagger(link, sums_of(halves))
            for spin in range(2):
                ahead = aheads[spin]
                behind = [
                    tuple(lattice.shift(p, direction, False) for p in h) for h in behinds[spin]
                ]
                place, phase = REBUILD[direction][spin]
                for c in range(3):
                    total, diff = plus(ahead[c], behind[c]), minus(ahead[c], behind[c])
                    if upper[spin][c] is None:
                        upper[spin][c] = total
                    else:
                        upper[spin][c] = plus(upper[spin][c], total)
                    if lower[place][c] is None:
                        zero = jnp.zeros_like(diff[0])
                        lower[place][c] = add_phase((zero, zero), diff, phase)
                    else:
                        lower[place][c] = add_phase(lower[place][c], diff, phase)
        for chiral, hops in ((0, upper), (1, lower)):
            field = [spinor(2 * chiral + i // 3, i % 3) for i in range(6)]
            field = [(x, y, x + y) for x, y in field]
            for row in range(6):
                total = None
                for column in range(6):
                    place = chiral * 72 + row * 6 + column
                    a, b, ab = field[column]
                    terms = (
                        clover[place] * ab,
                        clover_sums[place] * b,
                        clover_sums[place + 36] * a,
                    )
                    total = terms if total is None else [x + y for x, y in zip(total, terms)]
                both, re, im = total
                place = vector * (2 * COMPS) + chiral * 6 + row
                out[place] = both - re - HOPPING * hops[row // 3][row % 3][0]
                out[place + COMPS] = both + im - HOPPING * hops[row // 3][row % 3][1]
        return carry

    lax.fori_loop(0, vectors, body, 0)


def rim_signs():
    count, here = lax.axis_size("ta"), lax.axis_index("ta")
    one = jnp.float32(1.0)
    return jnp.where(here == count - 1, -one, one), jnp.where(here == 0, -one, one)


def finish(lattice, links, part, rim_ahead, rim_behind, vector, signs, store):
    ahead_all = unpack_rim(lattice, rim_ahead, vector, True, signs[0])
    behind_all = unpack_rim(lattice, rim_behind, vector, False, signs[1])
    both = times_link(link_at(links, 3), sums_of([ahead_all[:3], ahead_all[3:]]))
    for spin in range(2):
        ahead = both[spin]
        behind = behind_all[3 * spin : 3 * spin + 3]
        for c in range(3):
            for ri in range(2):
                f, b = ahead[c][ri], behind[c][ri]
                place = vector * (2 * COMPS) + ri * COMPS + spin * 3 + c
                store(place, part[place] - HOPPING * (f + b))
                store(place + 6, -(part[place + 6] + HOPPING * (f - b)))


def middle_kernel(
    lattice, vectors, part, links, rim_ahead, rim_behind, out, ahead_ref, behind_ref
):
    lattice.masks()
    signs = rim_signs()

    def body(vector, carry):
        def store(place, value):
            out[place] = value

        finish(lattice, links, part, rim_ahead, rim_behind, vector, signs, store)
        pack_rim(lattice, load_spinor(out, vector), links, ahead_ref, behind_ref, vector)
        return carry

    lax.fori_loop(0, vectors, body, 0, unroll=2)


def two_halves(value):
    high = value.astype(jnp.bfloat16)
    return high, (value - high.astype(jnp.float32)).astype(jnp.bfloat16)


def spans(first, last):
    return [(i, min(2, last - i)) for i in range(first, last, 2)]


def beside(ref, block, count):
    return jnp.concatenate([ref[block + i] for i in range(count)], axis=1)


def halves_beside(ref, block, count):
    return jnp.concatenate(two_halves(beside(ref, block, count)), axis=0)


def correlate_kernel(
    lattice, size, kept, scale, part, links, rim_ahead, rim_behind, basis, applied, over, field,
):
    lattice.masks()
    signs = rim_signs()
    rows = lattice.rows

    def body(vector, carry):
        def store(place, value):
            field[place] = value

        finish(lattice, links, part, rim_ahead, rim_behind, vector, signs, store)
        return carry

    lax.fori_loop(0, size, body, 0, unroll=2)

    total = jnp.zeros((4 * size, 4 * kept), jnp.float32)
    for comp in range(COMPS):
        blocks_here = slice(comp * rows, (comp + 1) * rows)
        for ri in range(2):
            for first in range(0, size, 8):
                count = min(8, size - first)
                tiles = jnp.stack(
                    [field[(first + i) * 2 * COMPS + ri * COMPS + comp] for i in range(count)]
                )
                start = ri * size + first
                applied[blocks_here, start : start + count, :] = jnp.swapaxes(tiles, 0, 1)
        mine = jnp.concatenate([applied[comp * rows + i] for i in range(rows)], axis=1)
        kept_rows = jnp.concatenate([basis[comp * rows + i] for i in range(rows)], axis=1)
        total = total + lax.dot_general(
            jnp.concatenate(two_halves(mine), axis=0),
            kept_rows,
            (((1,), (1,)), ((), ())),
            preferred_element_type=jnp.float32,
        )
    total = total[: 2 * size] + total[2 * size :]
    total = total[:, : 2 * kept] + total[:, 2 * kept :]
    real, imag = total[:size], total[size:]
    real, imag = (
        scale * (real[:, :kept] + imag[:, kept:]),
        scale * (imag[:, :kept] - real[:, kept:]),
    )
    over[...] = packed(jnp.concatenate([real, imag], axis=0))


def partner(here, step, count):
    if count & (count - 1) == 0:
        return here ^ step
    return (here + step) % count


def source(here, step, count):
    if count & (count - 1) == 0:
        return here ^ step
    return (here + count - step) % count


def exchanged(values, axis):
    count = lax.axis_size(axis)
    out = [values[0]]
    for step in range(1, count):
        pairs = [(i, partner(i, step, count)) for i in range(count)]
        out.append(lax.ppermute(values[step], axis, pairs))
    return out


def summed(value, axis, radix):
    count = lax.axis_size(axis)
    if count & (count - 1):
        return lax.psum(value, axis)
    stride = 1
    while stride < count:
        size, radix = min(radix[0], count // stride), radix[1:] or radix
        total = value
        for step in range(1, size):
            moved = lax.ppermute(value, axis, [(i, i ^ (step * stride)) for i in range(count)])
            total = total + moved
        value = total
        stride *= size
    return value


def packed(value):
    count = LANES // value.shape[1]
    size = value.shape[0] // count
    return jnp.concatenate([value[i * size : (i + 1) * size] for i in range(count)], axis=1)


def unpacked(value, width):
    return jnp.concatenate(
        [value[:, i * width : (i + 1) * width] for i in range(LANES // width)], axis=0
    )


def weight_rows(real, imag):
    weight = jnp.concatenate(
        [jnp.concatenate([real, -imag], axis=1), jnp.concatenate([imag, real], axis=1)], axis=0
    )
    high, low = two_halves(weight)
    return jnp.concatenate(
        [jnp.concatenate([high, high], axis=1), jnp.concatenate([low, low], axis=1)], axis=0
    )


def weighted(weight, basis):
    both = jnp.dot(weight, basis, preferred_element_type=jnp.float32)
    half = both.shape[0] // 2
    return both[:half] + both[half:]


def project_kernel(groups, vectors, kept, ship, over, basis, *outs):
    here = lax.axis_index("ba")
    per = basis.shape[0] // groups
    mine = unpacked(over[...], kept)
    weight = weight_rows(mine[:vectors], mine[vectors:])
    size = 2 * vectors
    for step in range(groups):
        first = partner(here, step, groups) * per + ship
        for block, count in spans(0, per - ship):
            value = weighted(weight, beside(basis, first + block, count))
            for i in range(count):
                start = (block + i) * size
                outs[step][start : start + size, :] = value[:, i * LANES : (i + 1) * LANES]
        outs[step][(per - ship) * size :, :] = over[...]


def rest_kernel(groups, vectors, kept, ship, scale, over, basis, applied, *refs):
    parts, refs = refs[:groups], refs[groups:]
    pieces, (rest_ref, gram) = refs[:-2], refs[-2:]
    here = lax.axis_index("ba")
    per = basis.shape[0] // groups
    tall = 2 * vectors
    weights = []
    for step in range(groups if ship else 1):
        there = over[...] if step == 0 else parts[step][(per - ship) * tall :, :]
        there = unpacked(there, kept)
        weights.append(weight_rows(there[:vectors], there[vectors:]))
    full = None
    for block, count in spans(0, ship) + spans(ship, per):
        mine = here * per + block
        if block < ship:
            total = weighted(weights[0], beside(basis, mine, count))
            for weight, piece in zip(weights[1:], pieces):
                total = total + weighted(weight, halves_beside(piece, block, count))
        else:
            here_rows = slice((block - ship) * tall, (block - ship + count) * tall)
            total = parts[0][here_rows, :]
            for part in parts[1:]:
                total = total + part[here_rows, :]
            total = jnp.concatenate(
                [total[i * tall : (i + 1) * tall] for i in range(count)], axis=1
            )
        rest = beside(applied, mine, count) - total
        for i in range(count):
            rest_ref[block + i] = rest[:, i * LANES : (i + 1) * LANES]
        both = jnp.concatenate(two_halves(rest), axis=0)
        term = lax.dot_general(
            both, both, (((1,), (1,)), ((), ())), preferred_element_type=jnp.float32
        )
        full = term if full is None else full + term
    full = full[: 2 * vectors] + full[2 * vectors :]
    full = full[:, : 2 * vectors] + full[:, 2 * vectors :]
    real, imag = full[:vectors], full[vectors:]
    gram[:, :vectors] = scale * (real[:, :vectors] + imag[:, vectors:])
    gram[:, vectors:] = scale * (real[:, vectors:] - imag[:, :vectors])


def ortho_kernel(groups, vectors, gram, rest, *refs):
    here = lax.axis_index("ba")
    outs, work = refs[:-1], refs[-1]
    shape = (vectors, 2 * vectors)
    row = lax.broadcasted_iota(jnp.int32, shape, 0)
    lane = lax.broadcasted_iota(jnp.int32, shape, 1)
    unit = jnp.where(lane == row + vectors, 1.0, 0.0)
    re = jnp.where(lane < vectors, gram[...], unit)
    im = jnp.concatenate([gram[:, vectors:], jnp.zeros((vectors, vectors), jnp.float32)], axis=1)
    pivots = jnp.ones(shape, jnp.float32)
    link_re = link_im = jnp.zeros(shape, jnp.float32)
    for first in range(0, vectors, 2):
        second = first + 1
        row0 = re[first:second], im[first:second]
        row1 = re[second : second + 1], im[second : second + 1]
        x0 = [jnp.broadcast_to(x[:, first:second], shape) for x in (re, im)]
        x1 = [jnp.broadcast_to(x[:, second : second + 1], shape) for x in (re, im)]
        top, low = x0[0][first:second], x1[0][second : second + 1]
        b_re, b_im = x1[0][first:second], x1[1][first:second]
        square = b_re * b_re + b_im * b_im
        inverse = jnp.where(row > second, 1.0 / (top * low - square), 0.0)
        f0_re = (x0[0] * low - (x1[0] * b_re + x1[1] * b_im)) * inverse
        f0_im = (x0[1] * low - (x1[1] * b_re - x1[0] * b_im)) * inverse
        f1_re = (x1[0] * top - (x0[0] * b_re - x0[1] * b_im)) * inverse
        f1_im = (x1[1] * top - (x0[0] * b_im + x0[1] * b_re)) * inverse
        here_first, here_second = row == first, row == second
        share = 1.0 / top
        pivots = jnp.where(
            here_first, top, jnp.where(here_second, low - square * share, pivots)
        )
        link_re = jnp.where(here_second, b_re * share, link_re)
        link_im = jnp.where(here_second, -b_im * share, link_im)
        re, im = (
            re - ((f0_re * row0[0] - f0_im * row0[1]) + (f1_re * row1[0] - f1_im * row1[1])),
            im - ((f0_re * row0[1] + f0_im * row0[0]) + (f1_re * row1[1] + f1_im * row1[0])),
        )
    above_re, above_im = pltpu.roll(re, 1, 0), pltpu.roll(im, 1, 0)
    re, im = (
        re - (link_re * above_re - link_im * above_im),
        im - (link_re * above_im + link_im * above_re),
    )
    roots = 1.0 / jnp.sqrt(pivots)
    inv_re, inv_im = (re * roots)[:, vectors:], (im * roots)[:, vectors:]
    own = vectors // groups
    for group in range(groups):
        rows = slice(group * own, (group + 1) * own)
        work[group, :own, :vectors] = inv_re[rows]
        work[group, :own, vectors:] = inv_im[rows]
        work[group, own:, :vectors] = -inv_im[rows]
        work[group, own:, vectors:] = inv_re[rows]
    weight = jnp.concatenate(
        [work[partner(here, step, groups)] for step in range(groups)], axis=0
    )
    high, low = two_halves(weight)
    weight = jnp.concatenate(
        [jnp.concatenate([high, high], axis=1), jnp.concatenate([low, low], axis=1)], axis=0
    )
    for block, count in spans(0, rest.shape[0]):
        full = weighted(weight, halves_beside(rest, block, count))
        for step in range(groups):
            rows = slice(step * 2 * own, (step + 1) * 2 * own)
            for i in range(count):
                outs[step][block + i] = full[rows, i * LANES : (i + 1) * LANES]


def place_kernel(groups, own, rows, *refs):
    parts, out = refs[:groups], refs[groups]
    here = lax.axis_index("ba")
    per = parts[0].shape[0]
    for step in range(groups):
        first = source(here, step, groups) * per
        if per % rows:
            for block in range(per):
                for ri in range(2):
                    out[:, ri, first + block, :] = parts[step][block, ri * own : (ri + 1) * own, :]
        else:
            for block in range(0, per, rows):
                tile = jnp.swapaxes(parts[step][block : block + rows], 0, 1)
                there = pl.ds(pl.multiple_of(first + block, rows), rows)
                for ri in range(2):
                    out[:, ri, there, :] = tile[ri * own : (ri + 1) * own]


def call(kernel, outs, *args, scratch=(), flops=0, grant=6, remote=()):
    nbytes = sum(a.size * a.dtype.itemsize for a in (*args, *outs))
    spec = pl.BlockSpec(memory_space=pltpu.VMEM)
    anywhere = pl.BlockSpec(memory_space=pltpu.HBM)
    return pl.pallas_call(
        kernel,
        out_shape=tuple(outs),
        in_specs=[anywhere if i in remote else spec for i in range(len(args))],
        out_specs=tuple([spec] * len(outs)),
        scratch_shapes=list(scratch),
        compiler_params=pltpu.CompilerParams(vmem_limit_bytes=grant << 20),
        cost_estimate=pl.CostEstimate(flops=flops, bytes_accessed=nbytes, transcendentals=0),
    )(*args)


def shape_of(*dims):
    return jax.ShapeDtypeStruct(dims, jnp.float32)


def tiles_of(value, leading):
    slices, sites = value.shape[-2:]
    value = value.reshape(leading, slices, sites // LANES, LANES)
    return value.swapaxes(1, 2).reshape(leading, slices * sites // LANES, LANES)


def per_device(search_block, kept_basis, gauge_links, clover_term):
    vectors, kept = search_block.shape[0], kept_basis.shape[0]
    slices, sites = search_block.shape[-2:]
    groups, places = lax.axis_size("ba"), lax.axis_size("ta")
    lattice = Lattice(slices, sites)
    rows = lattice.rows
    blocks = COMPS * rows
    per = blocks // groups
    own = vectors // groups
    scale = 1.0 / (2 * COMPS * slices * sites * places)
    psi = tiles_of(search_block, vectors * 2 * COMPS)
    basis = tiles_of(kept_basis, kept * 2 * COMPS).reshape(kept, 2, blocks, LANES)
    ship = per * 11 // 24 if per % rows == 0 else 0
    links = tiles_of(gauge_links, 72)
    clover = tiles_of(clover_term, 144)
    rim = shape_of(vectors * COMPS // slices, rows, LANES)
    field = shape_of(vectors * 2 * COMPS, rows, LANES)
    work = vectors * rows * LANES
    in_hbm = functools.partial(pltpu.with_memory_space_constraint, memory_space=pltpu.HBM)

    def swap(ahead, behind):
        down = [(i, (i + places - 1) % places) for i in range(places)]
        up = [(i, (i + 1) % places) for i in range(places)]
        second = lax.ppermute(behind, "ta", up)
        return lax.ppermute(ahead, "ta", down), second

    def local(values):
        return call(
            functools.partial(local_kernel, lattice, vectors),
            (field,),
            values,
            links,
            clover,
            scratch=[pltpu.VMEM(links.shape, jnp.float32), pltpu.VMEM(clover.shape, jnp.float32)],
            flops=2000 * work,
        )[0]

    psi, links, ahead, behind, *pieces = call(
        functools.partial(open_kernel, lattice, groups, vectors, kept, ship),
        (field, shape_of(*links.shape), rim, rim)
        + (shape_of(max(ship, 1), 2 * kept, LANES),) * (groups - 1),
        in_hbm(psi),
        in_hbm(links),
        in_hbm(basis),
        scratch=[
            pltpu.VMEM((groups - 1, kept, 2, -(-ship // rows) * rows or rows, LANES), jnp.float32),
            pltpu.SemaphoreType.DMA((groups + CHUNKS,)),
        ],
        flops=400 * work,
        grant=8,
        remote=(0, 1, 2),
    )
    rims = swap(ahead, behind)
    pieces = exchanged([None, *pieces], "ba")[1:] if ship else []
    part = local(psi)
    first, ahead, behind = call(
        functools.partial(middle_kernel, lattice, vectors),
        (field, rim, rim),
        part,
        links,
        *rims,
        flops=400 * work,
    )
    rims = swap(ahead, behind)
    (basis_rows,) = call(
        functools.partial(basis_kernel, rows, kept),
        (jax.ShapeDtypeStruct((blocks, 4 * kept, LANES), jnp.bfloat16),),
        basis,
    )
    part = local(first)
    applied, over = call(
        functools.partial(correlate_kernel, lattice, vectors, kept, scale),
        (shape_of(blocks, 2 * vectors, LANES), shape_of(2 * vectors * kept // LANES, LANES)),
        part,
        links,
        *rims,
        basis_rows,
        scratch=[pltpu.VMEM(psi.shape, jnp.float32)],
        flops=400 * work,
    )
    over = summed(over, "ta", (2, 4))
    parts = call(
        functools.partial(project_kernel, groups, vectors, kept, ship),
        (shape_of((per - ship) * 2 * vectors + over.shape[0], LANES),) * groups,
        over,
        basis_rows,
    )
    parts = exchanged(parts, "ba")
    rest, gram = call(
        functools.partial(rest_kernel, groups, vectors, kept, ship, scale),
        (shape_of(per, 2 * vectors, LANES), shape_of(vectors, 2 * vectors)),
        over,
        basis_rows,
        applied,
        *parts,
        *pieces,
    )
    gram = summed(gram, "ta", (2, 4))
    gram = summed(gram, "ba", (4,))
    piece = shape_of(per, 2 * own, LANES)
    pieces = call(
        functools.partial(ortho_kernel, groups, vectors),
        (piece,) * groups,
        gram,
        rest,
        scratch=[pltpu.VMEM((groups, 2 * own, 2 * vectors), jnp.float32)],
    )
    pieces = exchanged(pieces, "ba")
    (ortho,) = call(
        functools.partial(place_kernel, groups, own, rows),
        (shape_of(own, 2, blocks, LANES),),
        *pieces,
    )
    ortho = ortho.reshape(own * 2 * COMPS, sites // LANES, slices, LANES).swapaxes(1, 2)
    ortho = ortho.reshape(own, *search_block.shape[1:])
    over = over.reshape(over.shape[0], LANES // kept, kept).swapaxes(0, 1)
    return ortho, over.reshape(2, vectors, kept).swapaxes(1, 2)


def solution(mesh):
    placed = (
        P(None, None, None, None, "ta", None),
        P("ba", None, None, None, "ta", None),
        P(None, None, None, None, "ta", None),
        P(None, None, None, None, "ta", None),
    )


    return jax.shard_map(
        per_device,
        mesh=mesh,
        in_specs=placed,
        out_specs=(P("ba", None, None, None, "ta", None), P(None, "ba", None)),
        check_vma=False,
    )
```
